32 devices in a mesh: tm: 8 (over z, core), space: 4 (over y, x).
Axes of the slice: x: 2, y: 2, z: 4, core: 2. Of those that a mesh axis runs over, the one named last changes fastest.
Arguments:
- solution: float32 [512, 384, 384], P('tm', 'space'), may hold values from -6 to 6
- residual: float32 [512, 384, 384], P('tm', 'space'), may hold values from -6 to 6
- direction: float32 [512, 384, 384], P('tm', 'space'), may hold values from -6 to 6
- reaction: float32 [512, 384, 384], P('tm', 'space'), may hold values from 0.1 to 2
- time_bands: float32 [2, 4, 512], replicated, may hold values from -0.25 to 1.1, as said below
- space_bands: float32 [2, 4, 384], replicated, may hold values from -0.25 to 1.1, as said below
- time_basis: float32 [512, 512], replicated, may hold values from -0.25 to 0.25
- space_basis: float32 [384, 384], replicated, may hold values from -0.3125 to 0.3125
- time_eigen: float32 [512], replicated, may hold values from 0.1 to 1
- space_eigen: float32 [384], replicated, may hold values from 0.1 to 1
Outputs:
- new_solution: float32 [512, 384, 384], P('tm', 'space')
- new_residual: float32 [512, 384, 384], P('tm', 'space')
- new_direction: float32 [512, 384, 384], P('tm', 'space')
The draws below stay inside these ranges and needn't reach their ends.
Inputs may be any that keep to these rules, and one draw needn't show every extreme that they name: `time_bands`: each of the two matrices is symmetric with every diagonal entry larger than the sum of the magnitudes of the other entries of its row. `space_bands`: each of the two matrices is symmetric with every diagonal entry larger than the sum of the magnitudes of the other entries of its row.
All inputs are finite; a program needn't handle non-finite values.
Results may differ from the reference program's by a relative error of at most 0.000051.
Values sent between devices are 32-bit elements; how exact they have to be, the bound alone decides.
No kernel may reach another device: no remote copies, remote signals or barrier semaphores. Data moves between devices by JAX's collectives and lax.ppermute only.
A program may use at most 192 MiB of HBM per device.

```python
import math
import jax
import jax.numpy as jnp
from jax import lax

NT = 512
NS = 384


def band_table(key, length):
    subkeys = jax.random.split(key, 8)
    tables = []
    for matrix_index in range(2):
        diagonal = jax.random.uniform(subkeys[4 * matrix_index], (length,), jnp.float32, 0.9, 1.1)
        near_band = jax.random.uniform(subkeys[4 * matrix_index + 1], (length,), jnp.float32, -0.25, 0.25)
        middle_band = jax.random.uniform(subkeys[4 * matrix_index + 2], (length,), jnp.float32, -0.12, 0.12)
        outer_band = jax.random.uniform(subkeys[4 * matrix_index + 3], (length,), jnp.float32, -0.05, 0.05)
        tables.append(jnp.stack([diagonal, near_band, middle_band, outer_band]))
    return jnp.stack(tables)


def draw_time_bands(key, part):
    return band_table(jax.random.fold_in(key, 11), NT)


def draw_space_bands(key, part):
    return band_table(jax.random.fold_in(key, 23), NS)


def shard_levels(own_key, shape, pieces, smallest, top_value):
    loudness, own = 1.0, jax.random.fold_in(own_key, 6)
    for axis_at, parts in pieces:
        draws = jnp.exp(jax.random.uniform(jax.random.fold_in(own, axis_at), (parts,), jnp.float32, smallest / len(pieces), top_value / len(pieces)))
        loudness = loudness * jnp.repeat(draws, shape[axis_at] // parts).reshape([-1 if axis == axis_at else 1 for axis in range(len(shape))])
    return loudness


def centred(key, shape, width, bound, pieces=(), kind=jnp.bfloat16):
    entries = width * jax.random.normal(key, shape, jnp.float32)
    if pieces:
        entries = entries * shard_levels(key, shape, pieces, -0.22, 0.18)
    return jnp.clip(entries, -bound, bound).astype(kind)


def setup_inputs(seed: int = 0) -> dict:
    key_list = jax.random.split(jax.random.key(seed), 11)
    return {
        "solution": centred(key_list[0], (NT, NS, NS), 1.0, 6.0, ((0, 8), (1, 4)), jnp.float32),
        "residual": centred(key_list[1], (NT, NS, NS), 1.0, 6.0, ((0, 8), (1, 4)), jnp.float32),
        "direction": centred(key_list[2], (NT, NS, NS), 1.0, 6.0, ((0, 8), (1, 4)), jnp.float32),
        "reaction": jnp.clip(jnp.exp(math.log(2.0) - 2.9957323 * jax.random.uniform(key_list[3], (NT, NS, NS), jnp.float32) ** shard_levels(key_list[3], (NT, NS, NS), ((0, 8), (1, 4)), -0.2, 0.2)), 0.1, 2.0),
        "time_bands": draw_time_bands(jax.random.fold_in(key_list[10], 71), 0),
        "space_bands": draw_space_bands(jax.random.fold_in(key_list[10], 71), 0),
        "time_basis": centred(key_list[6], (NT, NT), NT ** -0.5, 0.25, (), jnp.float32),
        "space_basis": centred(key_list[7], (NS, NS), NS ** -0.5, 0.3125, (), jnp.float32),
        "time_eigen": jnp.clip(jnp.exp(jax.random.uniform(key_list[8], (NT,), jnp.float32, math.log(0.1), math.log(1.0))), 0.1, 1.0),
        "space_eigen": jnp.clip(jnp.exp(jax.random.uniform(key_list[9], (NS,), jnp.float32, math.log(0.1), math.log(1.0))), 0.1, 1.0),
    }


highest = lax.Precision.HIGHEST


def band_apply(extended, band_rows, dimension):
    length = extended.shape[dimension] - 6
    target_shape = [1] * extended.ndim
    target_shape[dimension] = length

    def coefficient(which_row, first_row):
        return lax.slice_in_dim(band_rows[which_row], first_row, first_row + length).reshape(target_shape)

    def window(first_row):
        return lax.slice_in_dim(extended, first_row, first_row + length, axis=dimension)

    result = coefficient(0, 3) * window(3)
    for offset in (1, 2, 3):
        result = result + coefficient(offset, 3) * window(3 + offset) + coefficient(offset, 3 - offset) * window(3 - offset)
    return result


def pad_along(values, dimension):
    widths = [(0, 0)] * values.ndim
    widths[dimension] = (3, 3)
    return jnp.pad(values, widths)


def apply_operator(direction, reaction, time_bands, space_bands):
    padded_time = jnp.pad(time_bands, ((0, 0), (0, 0), (3, 3)))
    padded_space = jnp.pad(space_bands, ((0, 0), (0, 0), (3, 3)))
    extended = pad_along(direction, 2)
    mass_y = band_apply(extended, padded_space[1], 2)
    stiff_y = band_apply(extended, padded_space[0], 2)
    mass_xy = band_apply(pad_along(mass_y, 1), padded_space[1], 1)
    stiff_x = band_apply(pad_along(mass_y, 1), padded_space[0], 1)
    stiff_yx = band_apply(pad_along(stiff_y, 1), padded_space[1], 1)
    temporal = band_apply(pad_along(mass_xy, 0), padded_time[0], 0) + band_apply(pad_along(stiff_x + stiff_yx, 0), padded_time[1], 0)
    return temporal + reaction * direction


def forward_transform(values, time_basis, space_basis):
    along_y = jnp.einsum('txk,ka->txa', values, space_basis, precision=highest)
    along_x = jnp.einsum('tjy,jb->tby', along_y, space_basis, precision=highest)
    return jnp.einsum('ixy,ia->axy', along_x, time_basis, precision=highest)


def inverse_transform(spectral, time_basis, space_basis):
    along_t = jnp.einsum('axy,ia->ixy', spectral, time_basis, precision=highest)
    along_x = jnp.einsum('tby,jb->tjy', along_t, space_basis, precision=highest)
    return jnp.einsum('txa,ka->txk', along_x, space_basis, precision=highest)


def reference(solution, residual, direction, reaction, time_bands, space_bands, time_basis, space_basis, time_eigen, space_eigen):
    image = apply_operator(direction, reaction, time_bands, space_bands)
    eigen_sum = time_eigen[:, None, None] + space_eigen[:, None] + space_eigen[None, :]
    first_hat = forward_transform(residual, time_basis, space_basis)
    norm_old = jnp.sum(first_hat * (first_hat / eigen_sum))
    curvature = jnp.sum(direction * image)
    step_size = norm_old / curvature
    new_solution = solution + step_size * direction
    new_residual = residual - step_size * image
    new_hat = forward_transform(new_residual, time_basis, space_basis)
    spectral = new_hat / eigen_sum
    norm_new = jnp.sum(new_hat * spectral)
    precond = inverse_transform(spectral, time_basis, space_basis)
    new_direction = precond + (norm_new / norm_old) * direction
    return new_solution, new_residual, new_direction
```

```python
import functools

import jax
import jax.numpy as jnp
from jax import lax
from jax.experimental import pallas as pl
from jax.experimental.pallas import tpu as pltpu
from jax.sharding import PartitionSpec as P


LANES = 128
f32 = jnp.float32
bf16 = jnp.bfloat16


def cost(flops, nbytes):
    return pl.CostEstimate(flops=int(flops), bytes_accessed=int(nbytes), transcendentals=0)


def params():
    return pltpu.CompilerParams(
        dimension_semantics=("arbitrary",), vmem_limit_bytes=40 * 1024 * 1024
    )


def halves(value):
    high = value.astype(bf16)
    return high, (value - high.astype(f32)).astype(bf16)


def halves_outside(value):
    high = lax.reduce_precision(value, 8, 7)
    return high.astype(bf16), (value - high).astype(bf16)


def dot(left, right):
    return jnp.dot(left, right, preferred_element_type=f32)


def dot_rows(left, right):
    return lax.dot_general(left, right, (((1,), (1,)), ((), ())), preferred_element_type=f32)


def dot3(left, right):
    return dot(left[0], right[0]) + (dot(left[0], right[1]) + dot(left[1], right[0]))


def swap_slots(arrays):
    count = len(arrays)
    width = LANES // count
    slot = lax.broadcasted_iota(jnp.int32, arrays[0].shape, 1) // width
    arrays = list(arrays)
    bit = 1
    while bit < count:
        upper = (slot & bit) != 0
        for i in range(count):
            if i & bit:
                continue
            low, high = arrays[i], arrays[i | bit]
            arrays[i] = jnp.where(upper, pltpu.roll(high, bit * width, 1), low)
            arrays[i | bit] = jnp.where(upper, high, pltpu.roll(low, LANES - bit * width, 1))
        bit *= 2
    return arrays


def y_forward_body(group, field_ref, weight_ref, *rest):
    outs, held = rest[:-1], rest[-1]
    rows, _, depth = field_ref.shape
    high, low = halves(field_ref[...].reshape(rows * group, depth))
    both = dot_rows(high, weight_ref[...])
    held[...] = both[:, :LANES] + (both[:, LANES:] + dot_rows(low, weight_ref[:LANES, :]))
    blocks = swap_slots([held[pl.ds(i, rows, stride=group), :] for i in range(group)])
    for out, block in zip(outs, blocks):
        out[0] = block


def y_forward(field, weight, group):
    rows, columns, depth = field.shape
    count = columns // group
    return pl.pallas_call(
        functools.partial(y_forward_body, group),
        grid=(count,),
        in_specs=[
            pl.BlockSpec((rows, group, depth), lambda g: (0, g, 0)),
            pl.BlockSpec((2 * LANES, depth), lambda g: (0, 0)),
        ],
        out_specs=[pl.BlockSpec((1, rows, LANES), lambda g: (g, 0, 0))] * group,
        out_shape=[jax.ShapeDtypeStruct((count, rows, LANES), f32)] * group,
        scratch_shapes=[pltpu.VMEM((rows * group, LANES), f32)],
        compiler_params=params(),
        cost_estimate=cost(
            6 * rows * columns * depth * LANES, 4 * rows * columns * (depth + LANES)
        ),
        name="y_forward",
    )(field, weight)


def t_forward_body(group, per_step, shares, *refs):
    parts, high_ref, low_ref, outs = refs[:group], refs[group], refs[group + 1], refs[group + 2 :]
    data = jnp.concatenate(
        [jnp.concatenate([part[i] for part in parts], axis=0) for i in range(per_step)], axis=1
    )
    result = dot3((high_ref[...], low_ref[...]), halves(data))
    owned = result.shape[0] // shares
    for f, out in enumerate(outs):
        for i in range(per_step):
            block = result[f * owned : (f + 1) * owned, i * LANES : (i + 1) * LANES]
            out[:, i * group : (i + 1) * group, :] = block.reshape(owned // group, group, LANES)


def t_forward(parts, high, low, shares):
    group = len(parts)
    count, rows, _ = parts[0].shape
    total = high.shape[0]
    owned = total // shares
    per_step = 2 if count % 2 == 0 else 1
    return pl.pallas_call(
        functools.partial(t_forward_body, group, per_step, shares),
        grid=(count // per_step,),
        in_specs=[pl.BlockSpec((per_step, rows, LANES), lambda g: (g, 0, 0))] * group
        + [pl.BlockSpec((total, total), lambda g: (0, 0))] * 2,
        out_specs=[pl.BlockSpec((owned // group, per_step * group, LANES), lambda g: (0, g, 0))]
        * shares,
        out_shape=[jax.ShapeDtypeStruct((owned // group, count * group, LANES), f32)] * shares,
        compiler_params=params(),
        cost_estimate=cost(6 * total * total * count * LANES, 8 * total * count * LANES),
        name="t_forward",
    )(*parts, high, low)


def t_inverse_body(group, per_step, shares, *refs):
    parts, high_ref, low_ref, outs = (
        refs[:shares],
        refs[shares],
        refs[shares + 1],
        refs[shares + 2 :],
    )
    data = jnp.concatenate(
        [
            jnp.concatenate(
                [
                    part[:, i * group : (i + 1) * group, :].reshape(part.shape[0] * group, LANES)
                    for part in parts
                ],
                axis=0,
            )
            for i in range(per_step)
        ],
        axis=1,
    )
    result = dot3((high_ref[...], low_ref[...]), halves(data))
    rows = result.shape[0] // group
    for e, out in enumerate(outs):
        for i in range(per_step):
            out[i] = result[e * rows : (e + 1) * rows, i * LANES : (i + 1) * LANES]


def t_inverse(parts, high, low, group):
    shares = len(parts)
    bundles, lines, _ = parts[0].shape
    count = lines // group
    total = high.shape[0]
    rows = total // group
    per_step = 2 if count % 2 == 0 else 1
    return pl.pallas_call(
        functools.partial(t_inverse_body, group, per_step, shares),
        grid=(count // per_step,),
        in_specs=[pl.BlockSpec((bundles, per_step * group, LANES), lambda g: (0, g, 0))] * shares
        + [pl.BlockSpec((total, total), lambda g: (0, 0))] * 2,
        out_specs=[pl.BlockSpec((per_step, rows, LANES), lambda g: (g, 0, 0))] * group,
        out_shape=[jax.ShapeDtypeStruct((count, rows, LANES), f32)] * group,
        compiler_params=params(),
        cost_estimate=cost(6 * total * total * count * LANES, 8 * total * count * LANES),
        name="t_inverse",
    )(*parts, high, low)


def gathered(parts, held, group):
    lines = parts[0].shape[1]
    pieces = []
    for h in range(2):
        for f, part in enumerate(parts):
            held[f * lines : (f + 1) * lines, :] = part[h]
        spread = [
            held[pl.ds(i, held.shape[0] // group, stride=group), :] for i in range(group)
        ]
        pieces.append(jnp.concatenate(swap_slots(spread), axis=0))
    return jnp.concatenate(pieces, axis=1)


def folded(values):
    return values.reshape(values.shape[0] // 8, 8, values.shape[1]).sum(0)


def x_first_body(group, shares, *refs):
    parts = refs[:shares]
    high_ref, low_ref, lane_ref, column_ref, hat_ref, sum_ref, held = refs[shares:]
    hat = dot3((high_ref[...], low_ref[...]), halves(gathered(parts, held, group)))
    hat_ref[0] = hat
    eigen_sum = column_ref[...] + lane_ref[0]

    @pl.when(pl.program_id(0) == 0)
    def _():
        sum_ref[...] = jnp.zeros_like(sum_ref)

    sum_ref[...] += folded(hat * (hat / eigen_sum))


def x_first(parts, high, low, lane_eigen, column_eigen, group):
    shares = len(parts)
    bundles, lines, _ = parts[0].shape
    wide = high.shape[0]
    return pl.pallas_call(
        functools.partial(x_first_body, group, shares),
        grid=(bundles // 2,),
        in_specs=[pl.BlockSpec((2, lines, LANES), lambda g: (g, 0, 0))] * shares
        + [pl.BlockSpec((wide, wide), lambda g: (0, 0))] * 2
        + [
            pl.BlockSpec((1, 1, 2 * LANES), lambda g: (g, 0, 0)),
            pl.BlockSpec((wide, 1), lambda g: (0, 0)),
        ],
        out_specs=[
            pl.BlockSpec((1, wide, 2 * LANES), lambda g: (g, 0, 0)),
            pl.BlockSpec((8, 2 * LANES), lambda g: (0, 0)),
        ],
        out_shape=[
            jax.ShapeDtypeStruct((bundles // 2, wide, 2 * LANES), f32),
            jax.ShapeDtypeStruct((8, 2 * LANES), f32),
        ],
        scratch_shapes=[pltpu.VMEM((shares * lines, LANES), f32)],
        compiler_params=params(),
        cost_estimate=cost(
            6 * wide * wide * bundles * LANES, 8 * wide * bundles * LANES
        ),
        name="x_first",
    )(*parts, high, low, lane_eigen, column_eigen)


def x_second_body(group, shares, *refs):
    step_ref, parts = refs[0], refs[1 : 1 + shares]
    (
        forward_high,
        forward_low,
        back_high,
        back_low,
        lane_ref,
        column_ref,
        hat_ref,
    ) = refs[1 + shares : 8 + shares]
    outs, sum_ref, held = refs[8 + shares : -2], refs[-2], refs[-1]
    image_hat = dot3((forward_high[...], forward_low[...]), halves(gathered(parts, held, group)))
    new_hat = hat_ref[0] - step_ref[0] * image_hat
    spectral = new_hat / (column_ref[...] + lane_ref[0])

    @pl.when(pl.program_id(0) == 0)
    def _():
        sum_ref[...] = jnp.zeros_like(sum_ref)

    sum_ref[...] += folded(new_hat * spectral)
    back = dot3((back_high[...], back_low[...]), halves(spectral))
    lines = outs[0].shape[1]
    each = held.shape[0] // group
    for h in range(2):
        spread = swap_slots(
            [
                back[i * each : (i + 1) * each, h * LANES : (h + 1) * LANES]
                for i in range(group)
            ]
        )
        for i in range(group):
            held[pl.ds(i, each, stride=group), :] = spread[i]
        for f, out in enumerate(outs):
            out[h] = held[f * lines : (f + 1) * lines, :]


def x_second(step, parts, forward, back, lane_eigen, column_eigen, hat, group):
    shares = len(parts)
    bundles, lines, _ = parts[0].shape
    wide = forward[0].shape[0]
    return pl.pallas_call(
        functools.partial(x_second_body, group, shares),
        grid=(bundles // 2,),
        in_specs=[pl.BlockSpec(memory_space=pltpu.SMEM)]
        + [pl.BlockSpec((2, lines, LANES), lambda g: (g, 0, 0))] * shares
        + [pl.BlockSpec((wide, wide), lambda g: (0, 0))] * 4
        + [
            pl.BlockSpec((1, 1, 2 * LANES), lambda g: (g, 0, 0)),
            pl.BlockSpec((wide, 1), lambda g: (0, 0)),
            pl.BlockSpec((1, wide, 2 * LANES), lambda g: (g, 0, 0)),
        ],
        out_specs=[pl.BlockSpec((2, lines, LANES), lambda g: (g, 0, 0))] * shares
        + [pl.BlockSpec((8, 2 * LANES), lambda g: (0, 0))],
        out_shape=[jax.ShapeDtypeStruct((bundles, lines, LANES), f32)] * shares
        + [jax.ShapeDtypeStruct((8, 2 * LANES), f32)],
        scratch_shapes=[pltpu.VMEM((shares * lines, LANES), f32)],
        compiler_params=params(),
        cost_estimate=cost(
            12 * wide * wide * bundles * LANES, 12 * wide * bundles * LANES
        ),
        name="x_second",
    )(step, *parts, *forward, *back, lane_eigen, column_eigen, hat)


def y_inverse_body(group, chunks, scaled, *refs):
    scale_ref = refs[0]
    parts = refs[1 : 1 + chunks * group]
    high_ref, low_ref = refs[1 + chunks * group : 3 + chunks * group]
    bases, out, held = refs[3 + chunks * group : -2], refs[-2], refs[-1]
    rows = parts[0].shape[1]
    for k in range(chunks):
        spread = swap_slots([part[0] for part in parts[k * group : (k + 1) * group]])
        for i in range(group):
            held[k, pl.ds(i, rows, stride=group), :] = spread[i]
    data = jnp.concatenate([held[k] for k in range(chunks)], axis=1)
    result = dot3(halves(data), (high_ref[...], low_ref[...])).reshape(out.shape)
    if scaled:
        out[...] = (result + bases[0][...]) + scale_ref[0] * bases[1][...]
    else:
        out[...] = result


def y_inverse(scale, parts, high, low, bases, group):
    chunks = len(parts) // group
    count, rows, _ = parts[0].shape
    depth = high.shape[1]
    block = pl.BlockSpec((rows, group, depth), lambda g: (0, g, 0))
    return pl.pallas_call(
        functools.partial(y_inverse_body, group, chunks, bool(bases)),
        grid=(count,),
        in_specs=[pl.BlockSpec(memory_space=pltpu.SMEM)]
        + [pl.BlockSpec((1, rows, LANES), lambda g: (g, 0, 0))] * len(parts)
        + [pl.BlockSpec((chunks * LANES, depth), lambda g: (0, 0))] * 2
        + [block] * len(bases),
        out_specs=block,
        out_shape=jax.ShapeDtypeStruct((rows, count * group, depth), f32),
        scratch_shapes=[pltpu.VMEM((chunks, rows * group, LANES), f32)],
        compiler_params=params(),
        cost_estimate=cost(
            6 * rows * count * group * depth * chunks * LANES,
            4 * rows * count * group * (depth * (1 + len(bases)) + chunks * LANES),
        ),
        name="y_inverse",
    )(scale, *parts, high, low, *bases)


def image_body(coefficient_ref, extended_ref, edge_ref, y_high, y_low, x_high, x_low, direction_ref,
               reaction_ref, image_ref, sum_ref, mass_ring, stiff_ring):
    step = pl.program_id(0)
    _, columns, depth = extended_ref.shape
    tall = columns + edge_ref.shape[1]
    slot = lax.rem(2 * step, 8)
    planes = jnp.concatenate(
        [extended_ref[0], edge_ref[0], extended_ref[1], edge_ref[1]], axis=0
    )
    along_y = halves(dot3(halves(planes), (y_high[...], y_low[...])))
    both = (x_high[...], x_low[...])
    mass = (x_high[:columns, :], x_low[:columns, :])
    for p in range(2):
        rows = slice(p * tall, (p + 1) * tall)
        of_mass = dot3(both, (along_y[0][rows, :depth], along_y[1][rows, :depth]))
        of_stiff = dot3(mass, (along_y[0][rows, depth:], along_y[1][rows, depth:]))
        mass_ring[slot + p] = of_mass[:columns]
        stiff_ring[slot + p] = of_mass[columns:] + of_stiff

    @pl.when(step == 0)
    def _():
        sum_ref[...] = jnp.zeros_like(sum_ref)

    @pl.when(step >= 3)
    def _():
        for p in range(2):
            row = 2 * (step - 3) + p
            total = reaction_ref[p] * direction_ref[p]
            for o in range(7):
                place = lax.rem(row + o, 8)
                total = total + (
                    coefficient_ref[row * 14 + o] * mass_ring[place]
                    + coefficient_ref[row * 14 + 7 + o] * stiff_ring[place]
                )
            image_ref[p] = total
            sum_ref[...] += folded(direction_ref[p] * total)


def shifted(cells, axis, step):
    count = lax.axis_size(axis)
    if step > 0:
        return lax.ppermute(cells, axis, [(i, i + 1) for i in range(count - 1)])
    return lax.ppermute(cells, axis, [(i + 1, i) for i in range(count - 1)])


def band_dense(row_bands, column_bands, row_at, column_at):
    distance = column_at[None, :] - row_at[:, None]
    total = jnp.zeros(distance.shape, f32)
    for k in range(4):
        total = jnp.where(distance == k, row_bands[k][:, None], total)
        if k:
            total = jnp.where(distance == -k, column_bands[k][None, :], total)
    return total


def apply_operator(direction, reaction, time_bands, space_bands):
    rows, columns, depth = direction.shape
    extended = jnp.concatenate(
        [
            shifted(direction[rows - 3 :], "tm", 1),
            direction,
            shifted(direction[:3], "tm", -1),
        ],
        axis=0,
    )
    edge = jnp.concatenate(
        [
            shifted(extended[:, columns - 3 :], "space", 1),
            shifted(extended[:, :3], "space", -1),
            jnp.zeros((rows + 6, 10, depth), f32),
        ],
        axis=1,
    )
    whole = jnp.arange(depth)
    y_matrix = jnp.concatenate(
        [
            band_dense(space_bands[1], space_bands[1], whole, whole),
            band_dense(space_bands[0], space_bands[0], whole, whole),
        ],
        axis=1,
    )
    padded_space = jnp.pad(space_bands, ((0, 0), (0, 0), (3, 3)))
    near_x = lax.dynamic_slice_in_dim(
        padded_space, lax.axis_index("space") * columns, columns + 6, 2
    )
    row_at = jnp.arange(columns)
    column_at = jnp.concatenate(
        [row_at, jnp.arange(-3, 0), jnp.arange(columns, columns + 3), jnp.full((10,), -1000)]
    )
    x_columns = jnp.concatenate(
        [
            near_x[:, :, 3 : 3 + columns],
            near_x[:, :, :3],
            near_x[:, :, 3 + columns :],
            jnp.zeros((2, 4, 10), f32),
        ],
        axis=2,
    )
    x_matrix = jnp.concatenate(
        [
            band_dense(near_x[m, :, 3 : 3 + columns], x_columns[m], row_at, column_at)
            for m in (1, 0)
        ],
        axis=0,
    )
    padded_time = jnp.pad(time_bands, ((0, 0), (0, 0), (3, 3)))
    near_t = lax.dynamic_slice_in_dim(padded_time, lax.axis_index("tm") * rows, rows + 6, 2)
    table = jnp.stack(
        [
            near_t[m, abs(o), 3 + min(o, 0) : 3 + min(o, 0) + rows]
            for m in (0, 1)
            for o in range(-3, 4)
        ],
        axis=1,
    ).reshape(-1)
    y_parts = halves_outside(y_matrix)
    x_parts = halves_outside(x_matrix)
    tall = columns + 16
    fixed = lambda shape: pl.BlockSpec(shape, lambda g: (0, 0))
    plane = lambda height: pl.BlockSpec((2, height, depth), lambda g: (g, 0, 0))
    late = pl.BlockSpec((2, columns, depth), lambda g: (jnp.maximum(g - 3, 0), 0, 0))
    return pl.pallas_call(
        image_body,
        grid=((rows + 6) // 2,),
        in_specs=[
            pl.BlockSpec(memory_space=pltpu.SMEM),
            plane(columns),
            plane(16),
            fixed((depth, 2 * depth)),
            fixed((depth, 2 * depth)),
            fixed((2 * columns, tall)),
            fixed((2 * columns, tall)),
            late,
            late,
        ],
        out_specs=[late, fixed((8, depth))],
        out_shape=[
            jax.ShapeDtypeStruct((rows, columns, depth), f32),
            jax.ShapeDtypeStruct((8, depth), f32),
        ],
        scratch_shapes=[pltpu.VMEM((8, columns, depth), f32)] * 2,
        compiler_params=params(),
        cost_estimate=cost(
            12 * (rows + 6) * tall * depth * depth, 16 * rows * columns * depth
        ),
        name="image",
    )(table, extended, edge, *y_parts, *x_parts, direction, reaction)


def exchange(blocks, axis):
    count = len(blocks)
    received = {
        k: lax.ppermute(blocks[k], axis, [(j, j ^ k) for j in range(count)])
        for k in range(count - 1, 0, -1)
    }
    return [blocks[0]] + [received[k] for k in range(1, count)]


def by_partner(values, axis, dim):
    count = lax.axis_size(axis)
    me = lax.axis_index(axis)
    return jnp.concatenate(
        [lax.dynamic_slice_in_dim(values, me ^ k, 1, dim) for k in range(count)], axis=dim
    )


def per_device(
    solution,
    residual,
    direction,
    reaction,
    time_bands,
    space_bands,
    time_basis,
    space_basis,
    time_eigen,
    space_eigen,
):
    rows, columns, depth = residual.shape
    group = lax.axis_size("tm")
    shares = lax.axis_size("space")
    me_t = lax.axis_index("tm")
    me_s = lax.axis_index("space")
    total = time_basis.shape[0]
    owned = total // shares
    width = LANES // group
    chunks = depth // LANES
    bundles = owned // group

    columns_first = by_partner(
        space_basis.T.reshape(chunks, group, width, depth), "tm", 1
    ).reshape(chunks, LANES, depth)
    y_high, y_low = halves_outside(columns_first)
    y_weights = jnp.concatenate([y_high, y_low], axis=1)

    time_ordered = by_partner(
        by_partner(time_basis.reshape(group, rows, total), "tm", 0).reshape(
            total, shares, owned
        ),
        "space",
        1,
    ).reshape(total, total)
    t_back = halves_outside(time_ordered)
    t_ahead = halves_outside(time_ordered.T)

    rows_first = (
        by_partner(space_basis.reshape(shares, columns, depth), "space", 0)
        .reshape(shares, columns // group, group, depth)
        .transpose(2, 0, 1, 3)
        .reshape(shares * columns, depth)
    )
    x_back = halves_outside(rows_first)
    x_ahead = halves_outside(rows_first.T)

    own_time = lax.dynamic_slice_in_dim(time_eigen, me_s * owned, owned)
    own_space = lax.dynamic_slice_in_dim(
        space_eigen.reshape(chunks, group, width), me_t, 1, 1
    ).reshape(chunks, width)
    lane_eigen = (own_time[None, :, None] + own_space[:, None, :]).reshape(
        chunks, bundles // 2, 1, 2 * LANES
    )
    column_eigen = space_eigen[:, None]

    def ahead(field):
        sent = [exchange(y_forward(field, y_weights[k], group), "tm") for k in range(chunks)]
        return [
            exchange(t_forward(sent[k], *t_ahead, shares), "space") for k in range(chunks)
        ]

    image, curvature_parts = apply_operator(direction, reaction, time_bands, space_bands)
    first = [
        x_first(parts, *x_ahead, lane_eigen[k], column_eigen, group)
        for k, parts in enumerate(ahead(residual))
    ]
    norm_old, curvature = lax.psum(
        (sum(jnp.sum(part) for _, part in first), jnp.sum(curvature_parts)), ("tm", "space")
    )
    step_size = norm_old / curvature
    step = step_size.reshape(1)
    back, sums = [], []
    for k, parts in enumerate(ahead(image)):
        *blocks, part = x_second(
            step, parts, x_ahead, x_back, lane_eigen[k], column_eigen, first[k][0], group
        )
        sums.append(jnp.sum(part))
        returned = exchange(blocks, "space")
        back.append(exchange(t_inverse(returned, *t_back, group), "tm"))
    norm_new = lax.psum(sum(sums), ("tm", "space"))
    scale = (norm_new / norm_old).reshape(1)
    last = chunks - 1
    early = y_inverse(
        step,
        [part for parts in back[:last] for part in parts],
        y_high[:last].reshape(last * LANES, depth),
        y_low[:last].reshape(last * LANES, depth),
        (),
        group,
    )
    new_direction = y_inverse(
        scale, back[last], y_high[last], y_low[last], (early, direction), group
    )
    new_residual = residual - step_size * image
    new_solution = solution + step_size * direction
    return (new_solution, new_residual, new_direction)


def solution(mesh):
    return jax.shard_map(
        per_device,
        mesh=mesh,
        in_specs=(
            P("tm", "space", None),
            P("tm", "space", None),
            P("tm", "space", None),
            P("tm", "space", None),
            P(),
            P(),
            P(),
            P(),
            P(),
            P(),
        ),
        out_specs=(P("tm", "space", None), P("tm", "space", None), P("tm", "space", None)),
        check_vma=False,
    )
```

```python
import functools

import jax
import jax.numpy as jnp
from jax import lax
from jax.experimental import pallas as pl
from jax.experimental.pallas import tpu as pltpu
from jax.sharding import PartitionSpec as P


LANES = 128
f32 = jnp.float32
bf16 = jnp.bfloat16


def cost(flops, nbytes):
    return pl.CostEstimate(flops=int(flops), bytes_accessed=int(nbytes), transcendentals=0)


def params(mib):
    return pltpu.CompilerParams(
        dimension_semantics=("arbitrary",), vmem_limit_bytes=mib * 1024 * 1024
    )


def ordered_call(body, after, in_specs, mib=40, **rest):
    def gated(*refs):
        return body(*refs[len(after) :])

    call = pl.pallas_call(
        gated,
        in_specs=[pl.BlockSpec(memory_space=pl.ANY)] * len(after) + list(in_specs),
        compiler_params=params(mib),
        **rest,
    )
    return lambda *args: call(*after, *args)


def halves(value):
    high = value.astype(bf16)
    return high, (value - high.astype(f32)).astype(bf16)


def halves_outside(value):
    high = lax.reduce_precision(value, 8, 7)
    return high.astype(bf16), (value - high).astype(bf16)


def dot(left, right):
    return jnp.dot(left, right, preferred_element_type=f32)


def dot_rows(left, right):
    return lax.dot_general(left, right, (((1,), (1,)), ((), ())), preferred_element_type=f32)


def dot3(left, right):
    return dot(left[0], right[0]) + (dot(left[0], right[1]) + dot(left[1], right[0]))


def swap_slots(arrays):
    count = len(arrays)
    width = LANES // count
    slot = lax.broadcasted_iota(jnp.int32, arrays[0].shape, 1) // width
    arrays = list(arrays)
    bit = 1
    while bit < count:
        upper = (slot & bit) != 0
        for i in range(count):
            if i & bit:
                continue
            low, high = arrays[i], arrays[i | bit]
            arrays[i] = jnp.where(upper, pltpu.roll(high, bit * width, 1), low)
            arrays[i | bit] = jnp.where(upper, high, pltpu.roll(low, LANES - bit * width, 1))
        bit *= 2
    return arrays


def y_forward_body(group, field_ref, weight_ref, *rest):
    outs, held = rest[:-1], rest[-1]
    rows, _, depth = field_ref.shape
    high, low = halves(field_ref[...].reshape(rows * group, depth))
    both = dot_rows(jnp.concatenate([high, low], axis=1), weight_ref[...])
    held[...] = both[:, :LANES] + both[:, LANES:]
    blocks = swap_slots([held[pl.ds(i, rows, stride=group), :] for i in range(group)])
    for out, block in zip(outs, blocks):
        out[0] = block


def y_forward(field, weight, group, mib, after=()):
    rows, columns, depth = field.shape
    count = columns // group
    return ordered_call(
        functools.partial(y_forward_body, group),
        after,
        mib=mib,
        grid=(count,),
        in_specs=[
            pl.BlockSpec((rows, group, depth), lambda g: (0, g, 0)),
            pl.BlockSpec((2 * LANES, 2 * depth), lambda g: (0, 0)),
        ],
        out_specs=[pl.BlockSpec((1, rows, LANES), lambda g: (g, 0, 0))] * group,
        out_shape=[jax.ShapeDtypeStruct((count, rows, LANES), f32)] * group,
        scratch_shapes=[pltpu.VMEM((rows * group, LANES), f32)],
        cost_estimate=cost(
            6 * rows * columns * depth * LANES, 4 * rows * columns * (depth + LANES)
        ),
        name="y_forward",
    )(field, weight)


def partner_rows(me, k, size):
    return pl.ds(pl.multiple_of((me ^ k) * size, 8), size)


def t_forward_body(group, per_step, shares, place_ref, *refs):
    parts, high_ref, low_ref, outs = (
        refs[:group],
        refs[group],
        refs[group + 1],
        refs[group + 2 : -1],
    )
    held = refs[-1]
    rows, owned = held.shape[0] // group, held.shape[0] // shares
    for i in range(per_step):
        lanes = slice(i * LANES, (i + 1) * LANES)
        for e, part in enumerate(parts):
            held[partner_rows(place_ref[0], e, rows), lanes] = part[i]
    held[...] = dot3((high_ref[...], low_ref[...]), halves(held[...]))
    for i in range(per_step):
        lanes = slice(i * LANES, (i + 1) * LANES)
        for f, out in enumerate(outs):
            block = held[partner_rows(place_ref[1], f, owned), lanes]
            out[:, i * group : (i + 1) * group, :] = block.reshape(owned // group, group, LANES)


def t_forward(place, parts, high, low, shares, after=()):
    group = len(parts)
    count, rows, _ = parts[0].shape
    total = high.shape[0]
    owned = total // shares
    per_step = 2 if count % 2 == 0 else 1
    return ordered_call(
        functools.partial(t_forward_body, group, per_step, shares),
        after,
        grid=(count // per_step,),
        in_specs=[pl.BlockSpec(memory_space=pltpu.SMEM)]
        + [pl.BlockSpec((per_step, rows, LANES), lambda g: (g, 0, 0))] * group
        + [pl.BlockSpec((total, total), lambda g: (0, 0))] * 2,
        out_specs=[pl.BlockSpec((owned // group, per_step * group, LANES), lambda g: (0, g, 0))]
        * shares,
        out_shape=[jax.ShapeDtypeStruct((owned // group, count * group, LANES), f32)] * shares,
        cost_estimate=cost(6 * total * total * count * LANES, 8 * total * count * LANES),
        scratch_shapes=[pltpu.VMEM((total, per_step * LANES), f32)],
        name="t_forward",
    )(place, *parts, high, low)


def t_inverse_body(group, per_step, shares, place_ref, *refs):
    parts, high_ref, low_ref, outs = (
        refs[:shares],
        refs[shares],
        refs[shares + 1],
        refs[shares + 2 : -1],
    )
    held = refs[-1]
    rows, owned = held.shape[0] // group, held.shape[0] // shares
    for i in range(per_step):
        lanes = slice(i * LANES, (i + 1) * LANES)
        for f, part in enumerate(parts):
            held[partner_rows(place_ref[1], f, owned), lanes] = part[
                :, i * group : (i + 1) * group, :
            ].reshape(owned, LANES)
    held[...] = dot3((high_ref[...], low_ref[...]), halves(held[...]))
    for i in range(per_step):
        lanes = slice(i * LANES, (i + 1) * LANES)
        for e, out in enumerate(outs):
            out[i] = held[partner_rows(place_ref[0], e, rows), lanes]


def t_inverse(place, parts, high, low, group, after=()):
    shares = len(parts)
    bundles, lines, _ = parts[0].shape
    count = lines // group
    total = high.shape[0]
    rows = total // group
    per_step = 2 if count % 2 == 0 else 1
    return ordered_call(
        functools.partial(t_inverse_body, group, per_step, shares),
        after,
        grid=(count // per_step,),
        in_specs=[pl.BlockSpec(memory_space=pltpu.SMEM)]
        + [pl.BlockSpec((bundles, per_step * group, LANES), lambda g: (0, g, 0))] * shares
        + [pl.BlockSpec((total, total), lambda g: (0, 0))] * 2,
        out_specs=[pl.BlockSpec((per_step, rows, LANES), lambda g: (g, 0, 0))] * group,
        out_shape=[jax.ShapeDtypeStruct((count, rows, LANES), f32)] * group,
        cost_estimate=cost(6 * total * total * count * LANES, 8 * total * count * LANES),
        scratch_shapes=[pltpu.VMEM((total, per_step * LANES), f32)],
        name="t_inverse",
    )(place, *parts, high, low)


def gathered(me, parts, held, group):
    lines = parts[0].shape[1]
    pieces = []
    for h in range(2):
        for f, part in enumerate(parts):
            held[partner_rows(me, f, lines), :] = part[h]
        spread = [
            held[pl.ds(i, held.shape[0] // group, stride=group), :] for i in range(group)
        ]
        pieces.append(jnp.concatenate(swap_slots(spread), axis=0))
    return jnp.concatenate(pieces, axis=1)


def folded(values):
    return values.reshape(values.shape[0] // 8, 8, values.shape[1]).sum(0)


def x_first_body(group, shares, place_ref, *refs):
    parts = refs[:shares]
    high_ref, low_ref, lane_ref, column_ref, hat_ref, sum_ref, held = refs[shares:]
    hat = dot3((high_ref[...], low_ref[...]), halves(gathered(place_ref[1], parts, held, group)))
    hat_ref[0] = hat
    eigen_sum = column_ref[...] + lane_ref[0]

    @pl.when(pl.program_id(0) == 0)
    def _():
        sum_ref[...] = jnp.zeros_like(sum_ref)

    sum_ref[...] += folded(hat * (hat / eigen_sum))


def x_first(place, parts, high, low, lane_eigen, column_eigen, group, after=()):
    shares = len(parts)
    bundles, lines, _ = parts[0].shape
    wide = high.shape[0]
    return ordered_call(
        functools.partial(x_first_body, group, shares),
        after,
        grid=(bundles // 2,),
        in_specs=[pl.BlockSpec(memory_space=pltpu.SMEM)]
        + [pl.BlockSpec((2, lines, LANES), lambda g: (g, 0, 0))] * shares
        + [pl.BlockSpec((wide, wide), lambda g: (0, 0))] * 2
        + [
            pl.BlockSpec((1, 1, 2 * LANES), lambda g: (g, 0, 0)),
            pl.BlockSpec((wide, 1), lambda g: (0, 0)),
        ],
        out_specs=[
            pl.BlockSpec((1, wide, 2 * LANES), lambda g: (g, 0, 0)),
            pl.BlockSpec((8, 2 * LANES), lambda g: (0, 0)),
        ],
        out_shape=[
            jax.ShapeDtypeStruct((bundles // 2, wide, 2 * LANES), f32),
            jax.ShapeDtypeStruct((8, 2 * LANES), f32),
        ],
        scratch_shapes=[pltpu.VMEM((shares * lines, LANES), f32)],
        cost_estimate=cost(
            6 * wide * wide * bundles * LANES, 8 * wide * bundles * LANES
        ),
        name="x_first",
    )(place, *parts, high, low, lane_eigen, column_eigen)


def x_second_body(group, shares, *refs):
    place_ref, step_ref, parts, refs = refs[0], refs[1], refs[2 : 2 + shares], refs[1:]
    (
        forward_high,
        forward_low,
        back_high,
        back_low,
        lane_ref,
        column_ref,
        hat_ref,
    ) = refs[1 + shares : 8 + shares]
    outs, sum_ref, held = refs[8 + shares : -2], refs[-2], refs[-1]
    image_hat = dot3((forward_high[...], forward_low[...]), halves(gathered(place_ref[1], parts, held, group)))
    new_hat = hat_ref[0] - step_ref[0] * image_hat
    spectral = new_hat / (column_ref[...] + lane_ref[0])

    @pl.when(pl.program_id(0) == 0)
    def _():
        sum_ref[...] = jnp.zeros_like(sum_ref)

    sum_ref[...] += folded(new_hat * spectral)
    back = dot3((back_high[...], back_low[...]), halves(spectral))
    lines = outs[0].shape[1]
    each = held.shape[0] // group
    for h in range(2):
        spread = swap_slots(
            [
                back[i * each : (i + 1) * each, h * LANES : (h + 1) * LANES]
                for i in range(group)
            ]
        )
        for i in range(group):
            held[pl.ds(i, each, stride=group), :] = spread[i]
        for f, out in enumerate(outs):
            out[h] = held[partner_rows(place_ref[1], f, lines), :]


def x_second(place, step, parts, forward, back, lane_eigen, column_eigen, hat, group, after=()):
    shares = len(parts)
    bundles, lines, _ = parts[0].shape
    wide = forward[0].shape[0]
    return ordered_call(
        functools.partial(x_second_body, group, shares),
        after,
        grid=(bundles // 2,),
        in_specs=[pl.BlockSpec(memory_space=pltpu.SMEM)] * 2
        + [pl.BlockSpec((2, lines, LANES), lambda g: (g, 0, 0))] * shares
        + [pl.BlockSpec((wide, wide), lambda g: (0, 0))] * 4
        + [
            pl.BlockSpec((1, 1, 2 * LANES), lambda g: (g, 0, 0)),
            pl.BlockSpec((wide, 1), lambda g: (0, 0)),
            pl.BlockSpec((1, wide, 2 * LANES), lambda g: (g, 0, 0)),
        ],
        out_specs=[pl.BlockSpec((2, lines, LANES), lambda g: (g, 0, 0))] * shares
        + [pl.BlockSpec((8, 2 * LANES), lambda g: (0, 0))],
        out_shape=[jax.ShapeDtypeStruct((bundles, lines, LANES), f32)] * shares
        + [jax.ShapeDtypeStruct((8, 2 * LANES), f32)],
        scratch_shapes=[pltpu.VMEM((shares * lines, LANES), f32)],
        cost_estimate=cost(
            12 * wide * wide * bundles * LANES, 12 * wide * bundles * LANES
        ),
        name="x_second",
    )(place, step, *parts, *forward, *back, lane_eigen, column_eigen, hat)


def y_inverse_body(group, chunks, scaled, *refs):
    scale_ref = refs[0]
    parts = refs[1 : 1 + chunks * group]
    high_ref, low_ref = refs[1 + chunks * group : 3 + chunks * group]
    bases, out, held = refs[3 + chunks * group : -2], refs[-2], refs[-1]
    rows = parts[0].shape[1]
    for k in range(chunks):
        spread = swap_slots([part[0] for part in parts[k * group : (k + 1) * group]])
        for i in range(group):
            held[k, pl.ds(i, rows, stride=group), :] = spread[i]
    high, low = halves(jnp.concatenate([held[k] for k in range(chunks)], axis=1))
    result = dot(high, low_ref[...]) + dot(
        jnp.concatenate([high, low], axis=1),
        jnp.concatenate([high_ref[...], high_ref[...]], axis=0),
    )
    result = result.reshape(out.shape)
    out[...] = result + (scale_ref[0] * bases[0][...] if scaled else bases[0][...])


def y_inverse(scale, parts, high, low, bases, group, scaled, after=()):
    chunks = len(parts) // group
    count, rows, _ = parts[0].shape
    depth = high.shape[1]
    block = pl.BlockSpec((rows, group, depth), lambda g: (0, g, 0))
    return ordered_call(
        functools.partial(y_inverse_body, group, chunks, scaled),
        after,
        mib=60,
        grid=(count,),
        in_specs=[pl.BlockSpec(memory_space=pltpu.SMEM)]
        + [pl.BlockSpec((1, rows, LANES), lambda g: (g, 0, 0))] * len(parts)
        + [pl.BlockSpec((chunks * LANES, depth), lambda g: (0, 0))] * 2
        + [block] * len(bases),
        out_specs=block,
        out_shape=jax.ShapeDtypeStruct((rows, count * group, depth), f32),
        scratch_shapes=[pltpu.VMEM((chunks, rows * group, LANES), f32)],
        cost_estimate=cost(
            6 * rows * count * group * depth * chunks * LANES,
            4 * rows * count * group * (depth * (1 + len(bases)) + chunks * LANES),
        ),
        name="y_inverse",
    )(scale, *parts, high, low, *bases)


def update_body(step_ref, solution_ref, residual_ref, direction_ref, image_ref, one_ref, two_ref):
    step = step_ref[0]
    one_ref[...] = solution_ref[...] + step * direction_ref[...]
    two_ref[...] = residual_ref[...] - step * image_ref[...]


def update(step, solution, residual, direction, image, after=()):
    rows, columns, depth = solution.shape
    block = pl.BlockSpec((2, columns, depth), lambda g: (g, 0, 0))
    return ordered_call(
        update_body,
        after,
        grid=(rows // 2,),
        in_specs=[pl.BlockSpec(memory_space=pltpu.SMEM)] + [block] * 4,
        out_specs=[block] * 2,
        out_shape=[jax.ShapeDtypeStruct(solution.shape, f32)] * 2,
        cost_estimate=cost(4 * rows * columns * depth, 24 * rows * columns * depth),
        name="update",
    )(step, solution, residual, direction, image)


STRIDE = 4
RING = 3 * STRIDE


def image_body(blocks, coefficient_ref, front_ref, back_ref, own_ref, edge_ref, *refs):
    y_refs, (x_ref, direction_ref, reaction_ref) = refs[:blocks], refs[blocks : blocks + 3]
    image_ref, sum_ref, planes, mass_ring, stiff_ring = refs[blocks + 3 :]
    step, last = pl.program_id(0), pl.num_programs(0) - 1
    _, columns, depth = own_ref.shape
    edges = edge_ref.shape[1]
    tall = columns + edges

    def take(source):
        for p in range(STRIDE):
            planes[p * tall : p * tall + columns, :] = source[p]

    pl.when(step == 0)(lambda: take(front_ref))
    pl.when(step == last)(lambda: take(back_ref))
    pl.when(jnp.logical_and(step > 0, step < last))(lambda: take(own_ref))
    for p in range(STRIDE):
        planes[p * tall + columns : (p + 1) * tall, :] = edge_ref[p]

    high, low = halves(planes[...])
    mass, stiff = [], []
    for c in range(blocks):
        near = slice(max(c - 1, 0) * LANES, min(c + 2, blocks) * LANES)
        both = dot(
            jnp.concatenate([high[:, near], low[:, near], high[:, near]], axis=1), y_refs[c][...]
        )
        mass.append(both[:, :LANES])
        stiff.append(both[:, LANES:])
    mass, stiff = jnp.concatenate(mass, axis=1), jnp.concatenate(stiff, axis=1)
    stacked = jnp.concatenate(
        [
            jnp.concatenate([part[p * tall : (p + 1) * tall] for part in (mass, stiff)], axis=0)
            for p in range(STRIDE)
        ],
        axis=1,
    )
    high, low = halves(stacked)
    wide = dot(x_ref[...], high)
    result = (wide[: 2 * columns] + wide[2 * columns :]) + dot(x_ref[: 2 * columns, :], low)
    slot = lax.rem(step, 3) * STRIDE
    for p in range(STRIDE):
        mass_ring[slot + p] = result[:columns, p * depth : (p + 1) * depth]
        stiff_ring[slot + p] = result[columns:, p * depth : (p + 1) * depth]

    @pl.when(step == 0)
    def _():
        sum_ref[...] = jnp.zeros_like(sum_ref)

    @pl.when(step >= 2)
    def _():
        for p in range(STRIDE):
            row = STRIDE * (step - 2) + p
            total = reaction_ref[p] * direction_ref[p]
            for o in range(7):
                place = lax.rem(row + o + STRIDE - 3, RING)
                total = total + (
                    coefficient_ref[row * 14 + o] * mass_ring[place]
                    + coefficient_ref[row * 14 + 7 + o] * stiff_ring[place]
                )
            image_ref[p] = total
            sum_ref[...] += folded(direction_ref[p] * total)


def neighbours(head, tail, axis):
    count = lax.axis_size(axis)
    even = lax.axis_index(axis) % 2 == 0
    received = []
    for first, sent in ((0, jnp.where(even, tail, head)), (1, jnp.where(even, head, tail))):
        pairs = [(i, i + 1) for i in range(first, count - 1, 2)]
        received.append(lax.ppermute(sent, axis, pairs + [(b, a) for a, b in pairs]))
    return jnp.where(even, received[1], received[0]), jnp.where(even, received[0], received[1])


def band_dense(row_bands, column_bands, row_at, column_at):
    distance = column_at[None, :] - row_at[:, None]
    total = jnp.zeros(distance.shape, f32)
    for k in range(4):
        total = jnp.where(distance == k, row_bands[k][:, None], total)
        if k:
            total = jnp.where(distance == -k, column_bands[k][None, :], total)
    return total


def apply_operator(direction, halos, reaction, time_bands, space_bands, after):
    rows, columns, depth = direction.shape
    blocks = depth // LANES
    plane = jnp.zeros((1, columns, depth), f32)
    before = jnp.concatenate([plane, halos[0]], axis=0)
    behind = jnp.concatenate([halos[1], plane], axis=0)

    def with_halos(part):
        return jnp.concatenate([part(halos[0]), part(direction), part(halos[1])], axis=0)

    edge = jnp.concatenate(
        neighbours(
            with_halos(lambda cells: cells[:, :3]),
            with_halos(lambda cells: cells[:, columns - 3 :]),
            "space",
        ),
        axis=1,
    )
    edge = jnp.pad(edge, ((1, 1), (0, 10), (0, 0)))
    whole = jnp.arange(depth)
    y_high, y_low = zip(
        *(
            halves_outside(band_dense(space_bands[m], space_bands[m], whole, whole))
            for m in (1, 0)
        )
    )
    y_parts = []
    for c in range(blocks):
        near = slice(max(c - 1, 0) * LANES, min(c + 2, blocks) * LANES)
        own = slice(c * LANES, (c + 1) * LANES)
        top, bottom = (
            jnp.concatenate([matrix[near, own] for matrix in matrices], axis=1)
            for matrices in (y_high, y_low)
        )
        y_parts.append(jnp.concatenate([top, top, bottom], axis=0))
    padded_space = jnp.pad(space_bands, ((0, 0), (0, 0), (3, 3)))
    near_x = lax.dynamic_slice_in_dim(
        padded_space, lax.axis_index("space") * columns, columns + 6, 2
    )
    row_at = jnp.arange(columns)
    column_at = jnp.concatenate(
        [row_at, jnp.arange(-3, 0), jnp.arange(columns, columns + 3), jnp.full((10,), -1000)]
    )
    x_columns = jnp.concatenate(
        [
            near_x[:, :, 3 : 3 + columns],
            near_x[:, :, :3],
            near_x[:, :, 3 + columns :],
            jnp.zeros((2, 4, 10), f32),
        ],
        axis=2,
    )
    x_stiff, x_mass = (
        band_dense(near_x[m, :, 3 : 3 + columns], x_columns[m], row_at, column_at)
        for m in (0, 1)
    )
    x_matrix = jnp.concatenate(
        [
            jnp.concatenate([x_mass, jnp.zeros_like(x_mass)], axis=1),
            jnp.concatenate([x_stiff, x_mass], axis=1),
        ],
        axis=0,
    )
    x_matrix = jnp.concatenate(halves_outside(x_matrix), axis=0)
    padded_time = jnp.pad(time_bands, ((0, 0), (0, 0), (3, 3)))
    near_t = lax.dynamic_slice_in_dim(padded_time, lax.axis_index("tm") * rows, rows + 6, 2)
    table = jnp.stack(
        [
            near_t[m, abs(o), 3 + min(o, 0) : 3 + min(o, 0) + rows]
            for m in (0, 1)
            for o in range(-3, 4)
        ],
        axis=1,
    ).reshape(-1)
    tall = columns + 16
    steps = rows // STRIDE + 2
    fixed = lambda array: pl.BlockSpec(array.shape, lambda g: (0,) * array.ndim)
    own = lambda late: pl.BlockSpec(
        (STRIDE, columns, depth), lambda g: (jnp.clip(g - late, 0, steps - 3), 0, 0)
    )
    return ordered_call(
        functools.partial(image_body, blocks),
        after,
        mib=56,
        grid=(steps,),
        in_specs=[pl.BlockSpec(memory_space=pltpu.SMEM), fixed(before), fixed(behind), own(1)]
        + [pl.BlockSpec((STRIDE, 16, depth), lambda g: (g, 0, 0))]
        + [fixed(part) for part in y_parts]
        + [fixed(x_matrix), own(2), own(2)],
        out_specs=[own(2), pl.BlockSpec((8, depth), lambda g: (0, 0))],
        out_shape=[
            jax.ShapeDtypeStruct((rows, columns, depth), f32),
            jax.ShapeDtypeStruct((8, depth), f32),
        ],
        scratch_shapes=[pltpu.VMEM((STRIDE * tall, depth), f32)]
        + [pltpu.VMEM((RING, columns, depth), f32)] * 2,
        cost_estimate=cost(
            12 * (rows + 6) * tall * depth * depth, 16 * rows * columns * depth
        ),
        name="image",
    )(table, before, behind, direction, edge, *y_parts, x_matrix, direction, reaction)


def exchange(blocks, axis):
    count = len(blocks)
    received = {
        k: lax.ppermute(blocks[k], axis, [(j, j ^ k) for j in range(count)])
        for k in range(count - 1, 0, -1)
    }
    return [blocks[0]] + [received[k] for k in range(1, count)]


def total_over(scalars):
    row = lax.broadcasted_iota(jnp.int32, (8, LANES), 0)
    packed = jnp.zeros((8, LANES), f32)
    for i, scalar in enumerate(scalars):
        packed = jnp.where(row == i, scalar, packed)
    for axis in ("space", "tm"):
        packed = sum(exchange([packed] * lax.axis_size(axis), axis))
    return [packed[i, 0] for i in range(len(scalars))]


def by_partner(values, axis, dim):
    count = lax.axis_size(axis)
    me = lax.axis_index(axis)
    return jnp.concatenate(
        [lax.dynamic_slice_in_dim(values, me ^ k, 1, dim) for k in range(count)], axis=dim
    )


def per_device(
    solution,
    residual,
    direction,
    reaction,
    time_bands,
    space_bands,
    time_basis,
    space_basis,
    time_eigen,
    space_eigen,
):
    rows, columns, depth = residual.shape
    group = lax.axis_size("tm")
    shares = lax.axis_size("space")
    me_t = lax.axis_index("tm")
    me_s = lax.axis_index("space")
    total = time_basis.shape[0]
    owned = total // shares
    width = LANES // group
    chunks = depth // LANES
    bundles = owned // group

    columns_first = by_partner(
        space_basis.T.reshape(chunks, group, width, depth), "tm", 1
    ).reshape(chunks, LANES, depth)
    y_high, y_low = halves_outside(columns_first)
    y_weights = jnp.concatenate([y_high, y_low], axis=1)
    y_weights = jnp.concatenate([y_weights, y_weights], axis=2)

    place = jnp.stack([me_t, me_s]).astype(jnp.int32)
    t_back = halves_outside(time_basis)
    t_ahead = halves_outside(time_basis.T)

    rows_first = (
        space_basis.reshape(shares, columns // group, group, depth)
        .transpose(2, 0, 1, 3)
        .reshape(shares * columns, depth)
    )
    x_back = halves_outside(rows_first)
    x_ahead = halves_outside(rows_first.T)

    own_time = lax.dynamic_slice_in_dim(time_eigen, me_s * owned, owned)
    own_space = lax.dynamic_slice_in_dim(
        space_eigen.reshape(chunks, group, width), me_t, 1, 1
    ).reshape(chunks, width)
    lane_eigen = (own_time[None, :, None] + own_space[:, None, :]).reshape(
        chunks, bundles // 2, 1, 2 * LANES
    )
    column_eigen = space_eigen[:, None]

    chain = []

    def kernel(call, *args):
        result = call(*args, chain[:])
        chain[:] = [result[0] if isinstance(result, (list, tuple)) else result]
        return result

    def y_ahead(field, k, name):
        blocks = kernel(y_forward, field, y_weights[k], group, 60 if name == "r" and k == 0 else 40)
        return exchange(blocks, "tm")

    def t_ahead_of(parts):
        blocks = kernel(t_forward, place, parts, *t_ahead, shares)
        return exchange(blocks, "space")

    def x_first_of(parts, k):
        return kernel(x_first, place, parts, *x_ahead, lane_eigen[k], column_eigen, group)

    def x_second_of(parts, k):
        *blocks, part = kernel(
            x_second,
            place,
            step,
            parts,
            x_ahead,
            x_back,
            lane_eigen[k],
            column_eigen,
            first[k][0],
            group,
        )
        return exchange(blocks, "space"), jnp.sum(part)

    def t_back_of(parts):
        blocks = kernel(t_inverse, place, parts, *t_back, group)
        return exchange(blocks, "tm")

    last = chunks - 1
    halos = neighbours(direction[:3], direction[rows - 3 :], "tm")
    sent = [y_ahead(residual, k, "r") for k in range(chunks)]
    image, curvature_parts = kernel(
        apply_operator, direction, halos, reaction, time_bands, space_bands
    )
    spread = [t_ahead_of(sent[0])]
    image_sent, first = [], []
    image_sent.append(y_ahead(image, 0, "i"))
    spread.append(t_ahead_of(sent[1]))
    first.append(x_first_of(spread[0], 0))
    for k in range(1, last):
        image_sent.append(y_ahead(image, k, "i"))
        spread.append(t_ahead_of(sent[k + 1]))
        first.append(x_first_of(spread[k], k))
    first.append(x_first_of(spread[last], last))
    norm_old, curvature = total_over(
        (sum(jnp.sum(part) for _, part in first), jnp.sum(curvature_parts))
    )
    step_size = norm_old / curvature
    step = step_size.reshape(1)
    image_spread = [t_ahead_of(image_sent[0])]
    image_sent.append(y_ahead(image, last, "i"))
    returned, back, sums = [], [], []
    for k in range(chunks):
        parts, part = x_second_of(image_spread[k], k)
        returned.append(parts)
        sums.append(part)
        if k < last:
            image_spread.append(t_ahead_of(image_sent[k + 1]))
            back.append(t_back_of(returned[k]))
    (norm_new,) = total_over((sum(sums),))
    back.append(t_back_of(returned[last]))
    scale = (norm_new / norm_old).reshape(1)
    new_solution, new_residual = kernel(update, step, solution, residual, direction, image)
    partial = kernel(
        y_inverse,
        scale,
        [part for parts in back[:last] for part in parts],
        y_high[:last].reshape(last * LANES, depth),
        y_low[:last].reshape(last * LANES, depth),
        (direction,),
        group,
        True,
    )
    new_direction = kernel(
        y_inverse, scale, back[last], y_high[last], y_low[last], (partial,), group, False
    )
    return (new_solution, new_residual, new_direction)


def solution(mesh):
    return jax.shard_map(
        per_device,
        mesh=mesh,
        in_specs=(
            P("tm", "space", None),
            P("tm", "space", None),
            P("tm", "space", None),
            P("tm", "space", None),
            P(),
            P(),
            P(),
            P(),
            P(),
            P(),
        ),
        out_specs=(P("tm", "space", None), P("tm", "space", None), P("tm", "space", None)),
        check_vma=False,
    )
```

```python
import functools

import jax
import jax.numpy as jnp
from jax import lax
from jax.experimental import pallas as pl
from jax.experimental.pallas import tpu as pltpu
from jax.sharding import PartitionSpec as P


LANES = 128
f32 = jnp.float32
bf16 = jnp.bfloat16


def cost(flops, nbytes):
    return pl.CostEstimate(flops=int(flops), bytes_accessed=int(nbytes), transcendentals=0)


def params(mib):
    return pltpu.CompilerParams(
        vmem_limit_bytes=mib * 1024 * 1024
    )


def ordered_call(body, after, in_specs, mib=40, **rest):
    def gated(*refs):
        return body(*refs[len(after) :])

    call = pl.pallas_call(
        gated,
        in_specs=[pl.BlockSpec(memory_space=pl.ANY)] * len(after) + list(in_specs),
        compiler_params=params(mib),
        **rest,
    )
    return lambda *args: call(*after, *args)


def halves(value):
    high = value.astype(bf16)
    return high, (value - high.astype(f32)).astype(bf16)


def halves_outside(value):
    high = lax.reduce_precision(value, 8, 7)
    return high.astype(bf16), (value - high).astype(bf16)


def dot(left, right):
    return jnp.dot(left, right, preferred_element_type=f32)


def dot_rows(left, right):
    return lax.dot_general(left, right, (((1,), (1,)), ((), ())), preferred_element_type=f32)


def dot3(left, right):
    return dot(left[0], right[0]) + (dot(left[0], right[1]) + dot(left[1], right[0]))


def swap_slots(arrays):
    count = len(arrays)
    width = LANES // count
    slot = lax.broadcasted_iota(jnp.int32, arrays[0].shape, 1) // width
    arrays = list(arrays)
    bit = 1
    while bit < count:
        upper = (slot & bit) != 0
        for i in range(count):
            if i & bit:
                continue
            low, high = arrays[i], arrays[i | bit]
            arrays[i] = jnp.where(upper, pltpu.roll(high, bit * width, 1), low)
            arrays[i | bit] = jnp.where(upper, high, pltpu.roll(low, LANES - bit * width, 1))
        bit *= 2
    return arrays


def y_forward_body(group, field_ref, weight_ref, *rest):
    outs, held = rest[:-1], rest[-1]
    rows, _, depth = field_ref.shape
    high, low = halves(field_ref[...].reshape(rows * group, depth))
    both = dot_rows(jnp.concatenate([high, low], axis=1), weight_ref[...])
    held[...] = both[:, :LANES] + both[:, LANES:]
    blocks = swap_slots([held[pl.ds(i, rows, stride=group), :] for i in range(group)])
    for out, block in zip(outs, blocks):
        out[0] = block


def y_forward(field, weight, group, mib, after=()):
    rows, columns, depth = field.shape
    count = columns // group
    return ordered_call(
        functools.partial(y_forward_body, group),
        after,
        mib=mib,
        grid=(count,),
        in_specs=[
            pl.BlockSpec((rows, group, depth), lambda g: (0, g, 0)),
            pl.BlockSpec((2 * LANES, 2 * depth), lambda g: (0, 0)),
        ],
        out_specs=[pl.BlockSpec((1, rows, LANES), lambda g: (g, 0, 0))] * group,
        out_shape=[jax.ShapeDtypeStruct((count, rows, LANES), f32)] * group,
        scratch_shapes=[pltpu.VMEM((rows * group, LANES), f32)],
        cost_estimate=cost(
            6 * rows * columns * depth * LANES, 4 * rows * columns * (depth + LANES)
        ),
        name="y_forward",
    )(field, weight)


def partner_rows(me, k, size, piece=0, pieces=1):
    share = size // pieces
    return pl.ds(pl.multiple_of((me ^ k) * size + piece * share, 8), share)


def t_forward_body(group, per_step, shares, place_ref, *refs):
    parts, high_ref, low_ref, outs = (
        refs[:group],
        refs[group],
        refs[group + 1],
        refs[group + 2 : -1],
    )
    held = refs[-1]
    rows, owned = held.shape[0] // group, held.shape[0] // shares
    for i in range(per_step):
        lanes = slice(i * LANES, (i + 1) * LANES)
        for e, part in enumerate(parts):
            held[partner_rows(place_ref[0], e, rows), lanes] = part[i]
    held[...] = dot3((high_ref[...], low_ref[...]), halves(held[...]))
    for i in range(per_step):
        lanes = slice(i * LANES, (i + 1) * LANES)
        pieces = len(outs) // shares
        for f, out in enumerate(outs):
            block = held[partner_rows(place_ref[1], f % shares, owned, f // shares, pieces), lanes]
            out[:, i * group : (i + 1) * group, :] = block.reshape(-1, group, LANES)


def t_forward(place, parts, high, low, shares, pieces, after=()):
    group = len(parts)
    count, rows, _ = parts[0].shape
    total = high.shape[0]
    bundles = total // shares // group // pieces
    per_step = 2 if count % 2 == 0 else 1
    return ordered_call(
        functools.partial(t_forward_body, group, per_step, shares),
        after,
        grid=(count // per_step,),
        in_specs=[pl.BlockSpec(memory_space=pltpu.SMEM)]
        + [pl.BlockSpec((per_step, rows, LANES), lambda g: (g, 0, 0))] * group
        + [pl.BlockSpec((total, total), lambda g: (0, 0))] * 2,
        out_specs=[pl.BlockSpec((bundles, per_step * group, LANES), lambda g: (0, g, 0))]
        * (shares * pieces),
        out_shape=[jax.ShapeDtypeStruct((bundles, count * group, LANES), f32)]
        * (shares * pieces),
        cost_estimate=cost(6 * total * total * count * LANES, 8 * total * count * LANES),
        scratch_shapes=[pltpu.VMEM((total, per_step * LANES), f32)],
        name="t_forward",
    )(place, *parts, high, low)


def t_inverse_body(group, per_step, shares, halved, place_ref, *refs):
    count = shares * halved
    parts, high_ref, low_ref, outs = (
        refs[:count],
        refs[count],
        refs[count + 1],
        refs[count + 2 : -1],
    )
    held = refs[-1]
    rows, owned = held.shape[0] // group, held.shape[0] // shares
    for i in range(per_step):
        lanes = slice(i * LANES, (i + 1) * LANES)
        for f, part in enumerate(parts):
            rows_of = partner_rows(place_ref[1], f % shares, owned, f // shares, halved)
            held[rows_of, lanes] = part[:, i * group : (i + 1) * group, :].reshape(-1, LANES)
    held[...] = dot3((high_ref[...], low_ref[...]), halves(held[...]))
    for i in range(per_step):
        lanes = slice(i * LANES, (i + 1) * LANES)
        for e, out in enumerate(outs):
            out[i] = held[partner_rows(place_ref[0], e, rows), lanes]


def t_inverse(place, parts, high, low, group, piece, pieces, after=()):
    shares = lax.axis_size("space")
    halved = len(parts) // shares
    bundles, lines, _ = parts[0].shape
    count = lines // group
    total = high.shape[0]
    rows = total // group
    per_step = 2 if count % 2 == 0 else 1
    steps = count // per_step
    begin, end = (-(-steps * p // pieces) for p in (piece, piece + 1))
    count = (end - begin) * per_step
    return ordered_call(
        functools.partial(t_inverse_body, group, per_step, shares, halved),
        after,
        grid=(end - begin,),
        in_specs=[pl.BlockSpec(memory_space=pltpu.SMEM)]
        + [pl.BlockSpec((bundles, per_step * group, LANES), lambda g: (0, g + begin, 0))] * len(parts)
        + [pl.BlockSpec((total, total), lambda g: (0, 0))] * 2,
        out_specs=[pl.BlockSpec((per_step, rows, LANES), lambda g: (g, 0, 0))] * group,
        out_shape=[jax.ShapeDtypeStruct((count, rows, LANES), f32)] * group,
        cost_estimate=cost(6 * total * total * count * LANES, 8 * total * count * LANES),
        scratch_shapes=[pltpu.VMEM((total, per_step * LANES), f32)],
        name="t_inverse",
    )(place, *parts, high, low)


def gathered(me, parts, held, group):
    lines = parts[0].shape[1]
    pieces = []
    for h in range(2):
        for f, part in enumerate(parts):
            held[partner_rows(me, f, lines), :] = part[h]
        spread = [
            held[pl.ds(i, held.shape[0] // group, stride=group), :] for i in range(group)
        ]
        pieces.append(jnp.concatenate(swap_slots(spread), axis=0))
    return jnp.concatenate(pieces, axis=1)


def folded(values):
    return values.reshape(values.shape[0] // 8, 8, values.shape[1]).sum(0)


def x_first_body(group, shares, place_ref, *refs):
    parts = refs[:shares]
    high_ref, low_ref, lane_ref, column_ref, hat_ref, sum_ref, held = refs[shares:]
    hat = dot3((high_ref[...], low_ref[...]), halves(gathered(place_ref[1], parts, held, group)))
    hat_ref[0] = hat
    eigen_sum = column_ref[...] + lane_ref[0]

    @pl.when(pl.program_id(0) == 0)
    def _():
        sum_ref[...] = jnp.zeros_like(sum_ref)

    sum_ref[...] += folded(hat * (hat / eigen_sum))


def x_first(place, parts, high, low, lane_eigen, column_eigen, group, after=()):
    shares = len(parts)
    bundles, lines, _ = parts[0].shape
    wide = high.shape[0]
    return ordered_call(
        functools.partial(x_first_body, group, shares),
        after,
        grid=(bundles // 2,),
        in_specs=[pl.BlockSpec(memory_space=pltpu.SMEM)]
        + [pl.BlockSpec((2, lines, LANES), lambda g: (g, 0, 0))] * shares
        + [pl.BlockSpec((wide, wide), lambda g: (0, 0))] * 2
        + [
            pl.BlockSpec((1, 1, 2 * LANES), lambda g: (g, 0, 0)),
            pl.BlockSpec((wide, 1), lambda g: (0, 0)),
        ],
        out_specs=[
            pl.BlockSpec((1, wide, 2 * LANES), lambda g: (g, 0, 0)),
            pl.BlockSpec((8, 2 * LANES), lambda g: (0, 0)),
        ],
        out_shape=[
            jax.ShapeDtypeStruct((bundles // 2, wide, 2 * LANES), f32),
            jax.ShapeDtypeStruct((8, 2 * LANES), f32),
        ],
        scratch_shapes=[pltpu.VMEM((shares * lines, LANES), f32)],
        cost_estimate=cost(
            6 * wide * wide * bundles * LANES, 8 * wide * bundles * LANES
        ),
        name="x_first",
    )(place, *parts, high, low, lane_eigen, column_eigen)


def x_second_body(group, shares, *refs):
    place_ref, step_ref, parts, refs = refs[0], refs[1], refs[2 : 2 + shares], refs[1:]
    (
        forward_high,
        forward_low,
        back_high,
        back_low,
        lane_ref,
        column_ref,
        hat_ref,
    ) = refs[1 + shares : 8 + shares]
    outs, sum_ref, held = refs[8 + shares : -2], refs[-2], refs[-1]
    image_hat = dot3((forward_high[...], forward_low[...]), halves(gathered(place_ref[1], parts, held, group)))
    new_hat = hat_ref[0] - step_ref[0] * image_hat
    spectral = new_hat / (column_ref[...] + lane_ref[0])

    @pl.when(pl.program_id(0) == 0)
    def _():
        sum_ref[...] = jnp.zeros_like(sum_ref)

    sum_ref[...] += folded(new_hat * spectral)
    back = dot3((back_high[...], back_low[...]), halves(spectral))
    lines = outs[0].shape[1]
    each = held.shape[0] // group
    for h in range(2):
        spread = swap_slots(
            [
                back[i * each : (i + 1) * each, h * LANES : (h + 1) * LANES]
                for i in range(group)
            ]
        )
        for i in range(group):
            held[pl.ds(i, each, stride=group), :] = spread[i]
        for f, out in enumerate(outs):
            out[h] = held[partner_rows(place_ref[1], f, lines), :]


def x_second(place, step, parts, forward, back, lane_eigen, column_eigen, hat, group, begin, after=()):
    shares = len(parts)
    bundles, lines, _ = parts[0].shape
    wide = forward[0].shape[0]
    return ordered_call(
        functools.partial(x_second_body, group, shares),
        after,
        grid=(bundles // 2,),
        in_specs=[pl.BlockSpec(memory_space=pltpu.SMEM)] * 2
        + [pl.BlockSpec((2, lines, LANES), lambda g: (g, 0, 0))] * shares
        + [pl.BlockSpec((wide, wide), lambda g: (0, 0))] * 4
        + [
            pl.BlockSpec((1, 1, 2 * LANES), lambda g: (g + begin, 0, 0)),
            pl.BlockSpec((wide, 1), lambda g: (0, 0)),
            pl.BlockSpec((1, wide, 2 * LANES), lambda g: (g + begin, 0, 0)),
        ],
        out_specs=[pl.BlockSpec((2, lines, LANES), lambda g: (g, 0, 0))] * shares
        + [pl.BlockSpec((8, 2 * LANES), lambda g: (0, 0))],
        out_shape=[jax.ShapeDtypeStruct((bundles, lines, LANES), f32)] * shares
        + [jax.ShapeDtypeStruct((8, 2 * LANES), f32)],
        scratch_shapes=[pltpu.VMEM((shares * lines, LANES), f32)],
        cost_estimate=cost(
            12 * wide * wide * bundles * LANES, 12 * wide * bundles * LANES
        ),
        name="x_second",
    )(place, step, *parts, *forward, *back, lane_eigen, column_eigen, hat)


def y_inverse_body(group, chunks, scaled, *refs):
    scale_ref = refs[0]
    parts = refs[1 : 1 + chunks * group]
    high_ref, low_ref = refs[1 + chunks * group : 3 + chunks * group]
    base_ref, out, held = refs[3 + chunks * group :]
    rows = parts[0].shape[1]
    for k in range(chunks):
        spread = swap_slots([part[0] for part in parts[k * group : (k + 1) * group]])
        for i in range(group):
            held[k, pl.ds(i, rows, stride=group), :] = spread[i]
    high, low = halves(jnp.concatenate([held[k] for k in range(chunks)], axis=1))
    result = dot(high, low_ref[...]) + dot(
        jnp.concatenate([high, low], axis=1),
        jnp.concatenate([high_ref[...], high_ref[...]], axis=0),
    )
    result = result.reshape(out.shape)
    out[...] = result + (scale_ref[0] * base_ref[...] if scaled else base_ref[...])


def y_inverse(scale, parts, high, low, base, group, scaled, begin=0, after=()):
    chunks = len(parts) // group
    count, rows, _ = parts[0].shape
    depth = high.shape[1]
    block = pl.BlockSpec((rows, group, depth), lambda g: (0, g + begin, 0))
    return ordered_call(
        functools.partial(y_inverse_body, group, chunks, scaled),
        after,
        mib=60,
        grid=(count,),
        in_specs=[pl.BlockSpec(memory_space=pltpu.SMEM)]
        + [pl.BlockSpec((1, rows, LANES), lambda g: (g, 0, 0))] * len(parts)
        + [pl.BlockSpec((chunks * LANES, depth), lambda g: (0, 0))] * 2
        + [block],
        out_specs=block,
        out_shape=jax.ShapeDtypeStruct(base.shape, f32),
        scratch_shapes=[pltpu.VMEM((chunks, rows * group, LANES), f32)],
        input_output_aliases={} if scaled else {len(after) + len(parts) + 3: 0},
        cost_estimate=cost(
            6 * rows * count * group * depth * chunks * LANES,
            4 * rows * count * group * (2 * depth + chunks * LANES),
        ),
        name="y_inverse",
    )(scale, *parts, high, low, base)


def update_body(step_ref, solution_ref, residual_ref, direction_ref, image_ref, one_ref, two_ref):
    step = step_ref[0]
    one_ref[...] = solution_ref[...] + step * direction_ref[...]
    two_ref[...] = residual_ref[...] - step * image_ref[...]


def update(step, solution, residual, direction, image, after=()):
    rows, columns, depth = solution.shape
    block = pl.BlockSpec((2, columns, depth), lambda g: (g, 0, 0))
    return ordered_call(
        update_body,
        after,
        grid=(rows // 2,),
        in_specs=[pl.BlockSpec(memory_space=pltpu.SMEM)] + [block] * 4,
        out_specs=[block] * 2,
        out_shape=[jax.ShapeDtypeStruct(solution.shape, f32)] * 2,
        cost_estimate=cost(4 * rows * columns * depth, 24 * rows * columns * depth),
        name="update",
    )(step, solution, residual, direction, image)


STRIDE = 4
RING = 3 * STRIDE


def image_body(blocks, coefficient_ref, front_ref, back_ref, own_ref, edge_ref, *refs):
    y_refs, (x_ref, direction_ref, reaction_ref) = refs[:blocks], refs[blocks : blocks + 3]
    image_ref, sum_ref, planes, mass_ring, stiff_ring = refs[blocks + 3 :]
    step, last = pl.program_id(0), pl.num_programs(0) - 1
    _, columns, depth = own_ref.shape
    edges = edge_ref.shape[1]
    tall = columns + edges

    def take(source):
        for p in range(STRIDE):
            planes[p * tall : p * tall + columns, :] = source[p]

    pl.when(step == 0)(lambda: take(front_ref))
    pl.when(step == last)(lambda: take(back_ref))
    pl.when(jnp.logical_and(step > 0, step < last))(lambda: take(own_ref))
    for p in range(STRIDE):
        planes[p * tall + columns : (p + 1) * tall, :] = edge_ref[p]

    high, low = halves(planes[...])
    mass, stiff = [], []
    for c in range(blocks):
        near = slice(max(c - 1, 0) * LANES, min(c + 2, blocks) * LANES)
        both = dot(
            jnp.concatenate([high[:, near], low[:, near], high[:, near]], axis=1), y_refs[c][...]
        )
        mass.append(both[:, :LANES])
        stiff.append(both[:, LANES:])
    mass, stiff = jnp.concatenate(mass, axis=1), jnp.concatenate(stiff, axis=1)
    stacked = jnp.concatenate(
        [
            jnp.concatenate([part[p * tall : (p + 1) * tall] for part in (mass, stiff)], axis=0)
            for p in range(STRIDE)
        ],
        axis=1,
    )
    high, low = halves(stacked)
    wide = dot(x_ref[...], high)
    result = (wide[: 2 * columns] + wide[2 * columns :]) + dot(x_ref[: 2 * columns, :], low)
    slot = lax.rem(step, 3) * STRIDE
    for p in range(STRIDE):
        mass_ring[slot + p] = result[:columns, p * depth : (p + 1) * depth]
        stiff_ring[slot + p] = result[columns:, p * depth : (p + 1) * depth]

    @pl.when(step == 0)
    def _():
        sum_ref[...] = jnp.zeros_like(sum_ref)

    @pl.when(step >= 2)
    def _():
        @pl.loop(0, STRIDE)
        def _(p):
            row = STRIDE * (step - 2) + p
            total = reaction_ref[p] * direction_ref[p]
            for o in range(7):
                place = lax.rem(row + o + STRIDE - 3, RING)
                total = total + (
                    coefficient_ref[row * 14 + o] * mass_ring[place]
                    + coefficient_ref[row * 14 + 7 + o] * stiff_ring[place]
                )
            image_ref[p] = total
            sum_ref[...] += folded(direction_ref[p] * total)


def neighbours(head, tail, axis):
    count = lax.axis_size(axis)
    even = lax.axis_index(axis) % 2 == 0
    received = []
    for first, sent in ((0, jnp.where(even, tail, head)), (1, jnp.where(even, head, tail))):
        pairs = [(i, i + 1) for i in range(first, count - 1, 2)]
        received.append(lax.ppermute(sent, axis, pairs + [(b, a) for a, b in pairs]))
    return jnp.where(even, received[1], received[0]), jnp.where(even, received[0], received[1])


def band_dense(row_bands, column_bands, row_at, column_at):
    distance = column_at[None, :] - row_at[:, None]
    total = jnp.zeros(distance.shape, f32)
    for k in range(4):
        total = jnp.where(distance == k, row_bands[k][:, None], total)
        if k:
            total = jnp.where(distance == -k, column_bands[k][None, :], total)
    return total


def apply_operator(direction, halos, reaction, time_bands, space_bands, after):
    rows, columns, depth = direction.shape
    blocks = depth // LANES
    plane = jnp.zeros((1, columns, depth), f32)
    before = jnp.concatenate([plane, halos[0]], axis=0)
    behind = jnp.concatenate([halos[1], plane], axis=0)

    def with_halos(part):
        return jnp.concatenate([part(halos[0]), part(direction), part(halos[1])], axis=0)

    edge = jnp.concatenate(
        neighbours(
            with_halos(lambda cells: cells[:, :3]),
            with_halos(lambda cells: cells[:, columns - 3 :]),
            "space",
        ),
        axis=1,
    )
    edge = jnp.pad(edge, ((1, 1), (0, 10), (0, 0)))
    whole = jnp.arange(depth)
    y_high, y_low = zip(
        *(
            halves_outside(band_dense(space_bands[m], space_bands[m], whole, whole))
            for m in (1, 0)
        )
    )
    y_parts = []
    for c in range(blocks):
        near = slice(max(c - 1, 0) * LANES, min(c + 2, blocks) * LANES)
        own = slice(c * LANES, (c + 1) * LANES)
        top, bottom = (
            jnp.concatenate([matrix[near, own] for matrix in matrices], axis=1)
            for matrices in (y_high, y_low)
        )
        y_parts.append(jnp.concatenate([top, top, bottom], axis=0))
    padded_space = jnp.pad(space_bands, ((0, 0), (0, 0), (3, 3)))
    near_x = lax.dynamic_slice_in_dim(
        padded_space, lax.axis_index("space") * columns, columns + 6, 2
    )
    row_at = jnp.arange(columns)
    column_at = jnp.concatenate(
        [row_at, jnp.arange(-3, 0), jnp.arange(columns, columns + 3), jnp.full((10,), -1000)]
    )
    x_columns = jnp.concatenate(
        [
            near_x[:, :, 3 : 3 + columns],
            near_x[:, :, :3],
            near_x[:, :, 3 + columns :],
            jnp.zeros((2, 4, 10), f32),
        ],
        axis=2,
    )
    x_stiff, x_mass = (
        band_dense(near_x[m, :, 3 : 3 + columns], x_columns[m], row_at, column_at)
        for m in (0, 1)
    )
    x_matrix = jnp.concatenate(
        [
            jnp.concatenate([x_mass, jnp.zeros_like(x_mass)], axis=1),
            jnp.concatenate([x_stiff, x_mass], axis=1),
        ],
        axis=0,
    )
    x_matrix = jnp.concatenate(halves_outside(x_matrix), axis=0)
    padded_time = jnp.pad(time_bands, ((0, 0), (0, 0), (3, 3)))
    near_t = lax.dynamic_slice_in_dim(padded_time, lax.axis_index("tm") * rows, rows + 6, 2)
    table = jnp.stack(
        [
            near_t[m, abs(o), 3 + min(o, 0) : 3 + min(o, 0) + rows]
            for m in (0, 1)
            for o in range(-3, 4)
        ],
        axis=1,
    ).reshape(-1)
    tall = columns + 16
    steps = rows // STRIDE + 2
    fixed = lambda array: pl.BlockSpec(array.shape, lambda g: (0,) * array.ndim)
    own = lambda late: pl.BlockSpec(
        (STRIDE, columns, depth), lambda g: (jnp.clip(g - late, 0, steps - 3), 0, 0)
    )
    return ordered_call(
        functools.partial(image_body, blocks),
        after,
        mib=56,
        grid=(steps,),
        in_specs=[pl.BlockSpec(memory_space=pltpu.SMEM), fixed(before), fixed(behind), own(1)]
        + [pl.BlockSpec((STRIDE, 16, depth), lambda g: (g, 0, 0))]
        + [fixed(part) for part in y_parts]
        + [fixed(x_matrix), own(2), own(2)],
        out_specs=[own(2), pl.BlockSpec((8, depth), lambda g: (0, 0))],
        out_shape=[
            jax.ShapeDtypeStruct((rows, columns, depth), f32),
            jax.ShapeDtypeStruct((8, depth), f32),
        ],
        scratch_shapes=[pltpu.VMEM((STRIDE * tall, depth), f32)]
        + [pltpu.VMEM((RING, columns, depth), f32)] * 2,
        cost_estimate=cost(
            12 * (rows + 6) * tall * depth * depth, 16 * rows * columns * depth
        ),
        name="image",
    )(table, before, behind, direction, edge, *y_parts, x_matrix, direction, reaction)


def by_xor(block, axis, k):
    return lax.ppermute(block, axis, [(j, j ^ k) for j in range(lax.axis_size(axis))])


def exchange(blocks, axis):
    count = len(blocks)
    received = {k: by_xor(blocks[k], axis, k) for k in range(count - 1, 0, -1)}
    return [blocks[0]] + [received[k] for k in range(1, count)]


def gathered_totals(scalars):
    row = lax.broadcasted_iota(jnp.int32, (8, LANES), 0)
    packed = jnp.zeros((8, LANES), f32)
    for i, scalar in enumerate(scalars):
        packed = jnp.where(row == i, scalar, packed)
    for axis in ("space", "tm"):
        packed = packed + by_xor(packed, axis, 1)
        parts = [packed] + [by_xor(packed, axis, k) for k in range(lax.axis_size(axis) - 2, 0, -2)]
        packed = sum(parts) if axis == "space" else packed
    return parts


def scale_body(old_ref, *refs):
    total = refs[0][...]
    for ref in refs[1:-1]:
        total = total + ref[...]
    refs[-1][...] = total / old_ref[0]


def scale_kernel(old, parts, after=()):
    return ordered_call(
        scale_body,
        after,
        in_specs=[pl.BlockSpec(memory_space=pltpu.SMEM)]
        + [pl.BlockSpec(memory_space=pltpu.VMEM)] * len(parts),
        out_specs=pl.BlockSpec(memory_space=pltpu.VMEM),
        out_shape=jax.ShapeDtypeStruct((8, LANES), f32),
        cost_estimate=cost(8 * LANES * len(parts), 4096 * len(parts)),
        name="scale",
    )(old, *parts)


def by_partner(values, axis, dim):
    count = lax.axis_size(axis)
    me = lax.axis_index(axis)
    return jnp.concatenate(
        [lax.dynamic_slice_in_dim(values, me ^ k, 1, dim) for k in range(count)], axis=dim
    )


def per_device(
    solution,
    residual,
    direction,
    reaction,
    time_bands,
    space_bands,
    time_basis,
    space_basis,
    time_eigen,
    space_eigen,
):
    rows, columns, depth = residual.shape
    group = lax.axis_size("tm")
    shares = lax.axis_size("space")
    me_t = lax.axis_index("tm")
    me_s = lax.axis_index("space")
    total = time_basis.shape[0]
    owned = total // shares
    width = LANES // group
    chunks = depth // LANES
    bundles = owned // group

    columns_first = by_partner(
        space_basis.T.reshape(chunks, group, width, depth), "tm", 1
    ).reshape(chunks, LANES, depth)
    y_high, y_low = halves_outside(columns_first)
    y_weights = jnp.concatenate([y_high, y_low], axis=1)
    y_weights = jnp.concatenate([y_weights, y_weights], axis=2)

    place = jnp.stack([me_t, me_s]).astype(jnp.int32)
    t_back = halves_outside(time_basis)
    t_ahead = halves_outside(time_basis.T)

    rows_first = (
        space_basis.reshape(shares, columns // group, group, depth)
        .transpose(2, 0, 1, 3)
        .reshape(shares * columns, depth)
    )
    x_back = halves_outside(rows_first)
    x_ahead = halves_outside(rows_first.T)

    own_time = lax.dynamic_slice_in_dim(time_eigen, me_s * owned, owned)
    own_space = lax.dynamic_slice_in_dim(
        space_eigen.reshape(chunks, group, width), me_t, 1, 1
    ).reshape(chunks, width)
    lane_eigen = (own_time[None, :, None] + own_space[:, None, :]).reshape(
        chunks, bundles // 2, 1, 2 * LANES
    )
    column_eigen = space_eigen[:, None]

    chain = []

    def kernel(call, *args):
        result = call(*args, chain[:])
        chain[:] = [result[0] if isinstance(result, (list, tuple)) else result]
        return result

    def y_ahead(field, k, name):
        blocks = kernel(y_forward, field, y_weights[k], group, 60 if name == "r" and k == 0 else 40)
        return exchange(blocks, "tm")

    def t_ahead_of(parts, pieces=1):
        blocks = kernel(t_forward, place, parts, *t_ahead, shares, pieces)
        if pieces == 1:
            return exchange(blocks, "space")
        return [exchange(blocks[p * shares : (p + 1) * shares], "space") for p in range(pieces)]

    def x_first_of(parts, k):
        return kernel(x_first, place, parts, *x_ahead, lane_eigen[k], column_eigen, group)

    def x_second_of(parts, k, piece=0, pieces=1):
        *blocks, part = kernel(
            x_second,
            place,
            step,
            parts,
            x_ahead,
            x_back,
            lane_eigen[k],
            column_eigen,
            first[k][0],
            group,
            piece * (bundles // 2 // pieces),
        )
        return exchange(blocks, "space"), jnp.sum(part)

    def t_back_of(parts, piece=0, pieces=1):
        blocks = kernel(t_inverse, place, parts, *t_back, group, piece, pieces)
        return exchange(blocks, "tm")

    last = chunks - 1
    halos = neighbours(direction[:3], direction[rows - 3 :], "tm")
    sent = [y_ahead(residual, k, "r") for k in range(chunks)]
    image, curvature_parts = kernel(
        apply_operator, direction, halos, reaction, time_bands, space_bands
    )
    spread = [t_ahead_of(sent[0])]
    image_sent, first = [y_ahead(image, 0, "i")], []
    for k in range(1, chunks):
        spread.append(t_ahead_of(sent[k]))
        first.append(x_first_of(spread[k - 1], k - 1))
        if k < last:
            image_sent.append(y_ahead(image, k, "i"))
    first.append(x_first_of(spread[last], last))
    totals = sum(
        gathered_totals((sum(jnp.sum(part) for _, part in first), jnp.sum(curvature_parts)))
    )
    norm_old, curvature = totals[0, 0], totals[1, 0]
    step_size = norm_old / curvature
    step = step_size.reshape(1)
    image_spread = [t_ahead_of(image_sent[0])]
    image_sent += [y_ahead(image, k, "i") for k in range(len(image_sent), chunks)]
    returned, back, sums = [], [], []
    pieces = 2 if bundles % 4 == 0 else 1
    for k in range(last):
        parts, part = x_second_of(image_spread[k], k)
        returned.append(parts)
        sums.append(part)
        if k == 0 and last > 1:
            image_spread.append(t_ahead_of(image_sent[1]))
            back.append(t_back_of(returned[0]))
        if k + 2 < last:
            image_spread.append(t_ahead_of(image_sent[k + 2]))
        if k == last - 1:
            image_spread.append(t_ahead_of(image_sent[last], pieces))
        if k >= len(back):
            back.append(t_back_of(returned[k]))
    ready = image_spread[last] if pieces > 1 else [image_spread[last]]
    returned_last = []
    for piece, parts in enumerate(ready):
        parts, part = x_second_of(parts, last, piece, pieces)
        returned_last += parts
        sums.append(part)
    new_parts = gathered_totals((sum(sums),))
    back_last = t_back_of(returned_last)
    new_solution, new_residual = kernel(update, step, solution, residual, direction, image)
    scale = kernel(scale_kernel, norm_old.reshape(1), new_parts)[0, 0].reshape(1)
    partial = kernel(
        y_inverse,
        scale,
        [part for parts in back[:last] for part in parts],
        y_high[:last].reshape(last * LANES, depth),
        y_low[:last].reshape(last * LANES, depth),
        direction,
        group,
        True,
        0,
    )
    new_direction = y_inverse(
        scale, back_last, y_high[last], y_low[last], partial, group, False
    )
    return (new_solution, new_residual, new_direction)


def solution(mesh):
    return jax.shard_map(
        per_device,
        mesh=mesh,
        in_specs=(
            P("tm", "space", None),
            P("tm", "space", None),
            P("tm", "space", None),
            P("tm", "space", None),
            P(),
            P(),
            P(),
            P(),
            P(),
            P(),
        ),
        out_specs=(P("tm", "space", None), P("tm", "space", None), P("tm", "space", None)),
        check_vma=False,
    )
```

```python
import functools

import jax
import jax.numpy as jnp
from jax import lax
from jax.experimental import pallas as pl
from jax.experimental.pallas import tpu as pltpu
from jax.sharding import PartitionSpec as P


LANES = 128
f32 = jnp.float32
bf16 = jnp.bfloat16


def cost(flops, nbytes):
    return pl.CostEstimate(flops=int(flops), bytes_accessed=int(nbytes), transcendentals=0)


def params(mib):
    return pltpu.CompilerParams(
        vmem_limit_bytes=mib * 1024 * 1024
    )


def ordered_call(body, after, in_specs, mib=40, **rest):
    def gated(*refs):
        return body(*refs[len(after) :])

    call = pl.pallas_call(
        gated,
        in_specs=[pl.BlockSpec(memory_space=pl.ANY)] * len(after) + list(in_specs),
        compiler_params=params(mib),
        **rest,
    )
    return lambda *args: call(*after, *args)


def halves(value):
    high = value.astype(bf16)
    return high, (value - high.astype(f32)).astype(bf16)


def halves_outside(value):
    high = lax.reduce_precision(value, 8, 7)
    return high.astype(bf16), (value - high).astype(bf16)


def dot(left, right):
    return jnp.dot(left, right, preferred_element_type=f32)


def dot_rows(left, right):
    return lax.dot_general(left, right, (((1,), (1,)), ((), ())), preferred_element_type=f32)


def stacked_left(parts):
    return jnp.concatenate([parts[0], parts[1], parts[0]], axis=1)


def stacked_right(parts):
    return jnp.concatenate([parts[0], parts[0], parts[1]], axis=0)


def swap_slots(arrays):
    count = len(arrays)
    width = LANES // count
    slot = lax.broadcasted_iota(jnp.int32, arrays[0].shape, 1) // width
    arrays = list(arrays)
    bit = 1
    while bit < count:
        upper = (slot & bit) != 0
        for i in range(count):
            if i & bit:
                continue
            low, high = arrays[i], arrays[i | bit]
            arrays[i] = jnp.where(upper, pltpu.roll(high, bit * width, 1), low)
            arrays[i | bit] = jnp.where(upper, high, pltpu.roll(low, LANES - bit * width, 1))
        bit *= 2
    return arrays


def y_forward_body(group, field_ref, weight_ref, *rest):
    outs, held = rest[:-1], rest[-1]
    rows, _, depth = field_ref.shape
    high, low = halves(field_ref[...].reshape(rows * group, depth))
    both = dot_rows(jnp.concatenate([high, low], axis=1), weight_ref[...])
    held[...] = both[:, :LANES] + both[:, LANES:]
    blocks = swap_slots([held[pl.ds(i, rows, stride=group), :] for i in range(group)])
    for out, block in zip(outs, blocks):
        out[0] = block


def y_forward(field, weight, group, mib, after=()):
    rows, columns, depth = field.shape
    count = columns // group
    return ordered_call(
        functools.partial(y_forward_body, group),
        after,
        mib=mib,
        grid=(count,),
        in_specs=[
            pl.BlockSpec((rows, group, depth), lambda g: (0, g, 0)),
            pl.BlockSpec((2 * LANES, 2 * depth), lambda g: (0, 0)),
        ],
        out_specs=[pl.BlockSpec((1, rows, LANES), lambda g: (g, 0, 0))] * group,
        out_shape=[jax.ShapeDtypeStruct((count, rows, LANES), f32)] * group,
        scratch_shapes=[pltpu.VMEM((rows * group, LANES), f32)],
        cost_estimate=cost(
            6 * rows * columns * depth * LANES, 4 * rows * columns * (depth + LANES)
        ),
        name="y_forward",
    )(field, weight)


def partner_rows(me, k, size, piece=0, pieces=1):
    share = size // pieces
    return pl.ds(pl.multiple_of((me ^ k) * size + piece * share, 8), share)


def t_forward_body(group, per_step, shares, place_ref, *refs):
    parts, weight_ref, outs = refs[:group], refs[group], refs[group + 1 : -1]
    held = refs[-1]
    rows, owned = held.shape[0] // group, held.shape[0] // shares
    for i in range(per_step):
        lanes = slice(i * LANES, (i + 1) * LANES)
        for e, part in enumerate(parts):
            held[partner_rows(place_ref[0], e, rows), lanes] = part[i]
    held[...] = dot(weight_ref[...], stacked_right(halves(held[...])))
    for i in range(per_step):
        lanes = slice(i * LANES, (i + 1) * LANES)
        pieces = len(outs) // shares
        for f, out in enumerate(outs):
            block = held[partner_rows(place_ref[1], f % shares, owned, f // shares, pieces), lanes]
            out[:, i * group : (i + 1) * group, :] = block.reshape(-1, group, LANES)


def t_forward(place, parts, weight, shares, pieces, after=()):
    group = len(parts)
    count, rows, _ = parts[0].shape
    total = weight.shape[0]
    bundles = total // shares // group // pieces
    per_step = 2 if count % 2 == 0 else 1
    return ordered_call(
        functools.partial(t_forward_body, group, per_step, shares),
        after,
        grid=(count // per_step,),
        in_specs=[pl.BlockSpec(memory_space=pltpu.SMEM)]
        + [pl.BlockSpec((per_step, rows, LANES), lambda g: (g, 0, 0))] * group
        + [pl.BlockSpec((total, 3 * total), lambda g: (0, 0))],
        out_specs=[pl.BlockSpec((bundles, per_step * group, LANES), lambda g: (0, g, 0))]
        * (shares * pieces),
        out_shape=[jax.ShapeDtypeStruct((bundles, count * group, LANES), f32)]
        * (shares * pieces),
        cost_estimate=cost(6 * total * total * count * LANES, 8 * total * count * LANES),
        scratch_shapes=[pltpu.VMEM((total, per_step * LANES), f32)],
        name="t_forward",
    )(place, *parts, weight)


def t_inverse_body(group, per_step, shares, halved, place_ref, *refs):
    count = shares * halved
    parts, weight_ref, outs = refs[:count], refs[count], refs[count + 1 : -1]
    held = refs[-1]
    rows, owned = held.shape[0] // group, held.shape[0] // shares
    for i in range(per_step):
        lanes = slice(i * LANES, (i + 1) * LANES)
        for f, part in enumerate(parts):
            rows_of = partner_rows(place_ref[1], f % shares, owned, f // shares, halved)
            held[rows_of, lanes] = part[:, i * group : (i + 1) * group, :].reshape(-1, LANES)
    held[...] = dot(weight_ref[...], stacked_right(halves(held[...])))
    for i in range(per_step):
        lanes = slice(i * LANES, (i + 1) * LANES)
        for e, out in enumerate(outs):
            out[i] = held[partner_rows(place_ref[0], e, rows), lanes]


def t_inverse(place, parts, weight, group, piece, pieces, after=()):
    shares = lax.axis_size("space")
    halved = len(parts) // shares
    bundles, lines, _ = parts[0].shape
    count = lines // group
    total = weight.shape[0]
    rows = total // group
    per_step = 2 if count % 2 == 0 else 1
    steps = count // per_step
    begin, end = (-(-steps * p // pieces) for p in (piece, piece + 1))
    count = (end - begin) * per_step
    return ordered_call(
        functools.partial(t_inverse_body, group, per_step, shares, halved),
        after,
        grid=(end - begin,),
        in_specs=[pl.BlockSpec(memory_space=pltpu.SMEM)]
        + [pl.BlockSpec((bundles, per_step * group, LANES), lambda g: (0, g + begin, 0))] * len(parts)
        + [pl.BlockSpec((total, 3 * total), lambda g: (0, 0))],
        out_specs=[pl.BlockSpec((per_step, rows, LANES), lambda g: (g, 0, 0))] * group,
        out_shape=[jax.ShapeDtypeStruct((count, rows, LANES), f32)] * group,
        cost_estimate=cost(6 * total * total * count * LANES, 8 * total * count * LANES),
        scratch_shapes=[pltpu.VMEM((total, per_step * LANES), f32)],
        name="t_inverse",
    )(place, *parts, weight)


def gathered(me, parts, held, group):
    lines = parts[0].shape[1]
    pieces = []
    for h in range(2):
        for f, part in enumerate(parts):
            held[partner_rows(me, f, lines), :] = part[h]
        spread = [
            held[pl.ds(i, held.shape[0] // group, stride=group), :] for i in range(group)
        ]
        pieces.append(jnp.concatenate(swap_slots(spread), axis=0))
    return jnp.concatenate(pieces, axis=1)


def folded(values):
    return values.reshape(values.shape[0] // 8, 8, values.shape[1]).sum(0)


def x_first_body(group, shares, place_ref, *refs):
    parts = refs[:shares]
    weight_ref, lane_ref, column_ref, hat_ref, sum_ref, held = refs[shares:]
    hat = dot(weight_ref[...], stacked_right(halves(gathered(place_ref[1], parts, held, group))))
    hat_ref[0] = hat
    eigen_sum = column_ref[...] + lane_ref[0]

    @pl.when(pl.program_id(0) == 0)
    def _():
        sum_ref[...] = jnp.zeros_like(sum_ref)

    sum_ref[...] += folded(hat * (hat / eigen_sum))


def x_first(place, parts, weight, lane_eigen, column_eigen, group, after=()):
    shares = len(parts)
    bundles, lines, _ = parts[0].shape
    wide = weight.shape[0]
    return ordered_call(
        functools.partial(x_first_body, group, shares),
        after,
        grid=(bundles // 2,),
        in_specs=[pl.BlockSpec(memory_space=pltpu.SMEM)]
        + [pl.BlockSpec((2, lines, LANES), lambda g: (g, 0, 0))] * shares
        + [pl.BlockSpec((wide, 3 * wide), lambda g: (0, 0))]
        + [
            pl.BlockSpec((1, 1, 2 * LANES), lambda g: (g, 0, 0)),
            pl.BlockSpec((wide, 1), lambda g: (0, 0)),
        ],
        out_specs=[
            pl.BlockSpec((1, wide, 2 * LANES), lambda g: (g, 0, 0)),
            pl.BlockSpec((8, 2 * LANES), lambda g: (0, 0)),
        ],
        out_shape=[
            jax.ShapeDtypeStruct((bundles // 2, wide, 2 * LANES), f32),
            jax.ShapeDtypeStruct((8, 2 * LANES), f32),
        ],
        scratch_shapes=[pltpu.VMEM((shares * lines, LANES), f32)],
        cost_estimate=cost(
            6 * wide * wide * bundles * LANES, 8 * wide * bundles * LANES
        ),
        name="x_first",
    )(place, *parts, weight, lane_eigen, column_eigen)


def x_second_body(group, shares, *refs):
    place_ref, step_ref, parts, refs = refs[0], refs[1], refs[2 : 2 + shares], refs[1:]
    forward_ref, back_ref, lane_ref, column_ref, hat_ref = refs[1 + shares : 6 + shares]
    outs, sum_ref, held = refs[6 + shares : -2], refs[-2], refs[-1]
    image_hat = dot(
        forward_ref[...], stacked_right(halves(gathered(place_ref[1], parts, held, group)))
    )
    new_hat = hat_ref[0] - step_ref[0] * image_hat
    spectral = new_hat / (column_ref[...] + lane_ref[0])

    @pl.when(pl.program_id(0) == 0)
    def _():
        sum_ref[...] = jnp.zeros_like(sum_ref)

    sum_ref[...] += folded(new_hat * spectral)
    back = dot(back_ref[...], stacked_right(halves(spectral)))
    lines = outs[0].shape[1]
    each = held.shape[0] // group
    for h in range(2):
        spread = swap_slots(
            [
                back[i * each : (i + 1) * each, h * LANES : (h + 1) * LANES]
                for i in range(group)
            ]
        )
        for i in range(group):
            held[pl.ds(i, each, stride=group), :] = spread[i]
        for f, out in enumerate(outs):
            out[h] = held[partner_rows(place_ref[1], f, lines), :]


def x_second(place, step, parts, forward, back, lane_eigen, column_eigen, hat, group, begin, after=()):
    shares = len(parts)
    bundles, lines, _ = parts[0].shape
    wide = forward.shape[0]
    return ordered_call(
        functools.partial(x_second_body, group, shares),
        after,
        grid=(bundles // 2,),
        in_specs=[pl.BlockSpec(memory_space=pltpu.SMEM)] * 2
        + [pl.BlockSpec((2, lines, LANES), lambda g: (g, 0, 0))] * shares
        + [pl.BlockSpec((wide, 3 * wide), lambda g: (0, 0))] * 2
        + [
            pl.BlockSpec((1, 1, 2 * LANES), lambda g: (g + begin, 0, 0)),
            pl.BlockSpec((wide, 1), lambda g: (0, 0)),
            pl.BlockSpec((1, wide, 2 * LANES), lambda g: (g + begin, 0, 0)),
        ],
        out_specs=[pl.BlockSpec((2, lines, LANES), lambda g: (g, 0, 0))] * shares
        + [pl.BlockSpec((8, 2 * LANES), lambda g: (0, 0))],
        out_shape=[jax.ShapeDtypeStruct((bundles, lines, LANES), f32)] * shares
        + [jax.ShapeDtypeStruct((8, 2 * LANES), f32)],
        scratch_shapes=[pltpu.VMEM((shares * lines, LANES), f32)],
        cost_estimate=cost(
            12 * wide * wide * bundles * LANES, 12 * wide * bundles * LANES
        ),
        name="x_second",
    )(place, step, *parts, forward, back, lane_eigen, column_eigen, hat)


def y_inverse_body(group, chunks, scaled, *refs):
    scale_ref = refs[0]
    parts = refs[1 : 1 + chunks * group]
    weight_ref, base_ref, out, held = refs[1 + chunks * group :]
    rows = parts[0].shape[1]
    for k in range(chunks):
        spread = swap_slots([part[0] for part in parts[k * group : (k + 1) * group]])
        for i in range(group):
            held[k, pl.ds(i, rows, stride=group), :] = spread[i]
    data = jnp.concatenate([held[k] for k in range(chunks)], axis=1)
    result = dot(stacked_left(halves(data)), weight_ref[...])
    result = result.reshape(out.shape)
    out[...] = result + (scale_ref[0] * base_ref[...] if scaled else base_ref[...])


def y_inverse(scale, parts, weight, base, group, scaled, begin=0, after=()):
    chunks = len(parts) // group
    count, rows, _ = parts[0].shape
    depth = weight.shape[1]
    block = pl.BlockSpec((rows, group, depth), lambda g: (0, g + begin, 0))
    return ordered_call(
        functools.partial(y_inverse_body, group, chunks, scaled),
        after,
        mib=60,
        grid=(count,),
        in_specs=[pl.BlockSpec(memory_space=pltpu.SMEM)]
        + [pl.BlockSpec((1, rows, LANES), lambda g: (g, 0, 0))] * len(parts)
        + [pl.BlockSpec((3 * chunks * LANES, depth), lambda g: (0, 0))]
        + [block],
        out_specs=block,
        out_shape=jax.ShapeDtypeStruct(base.shape, f32),
        scratch_shapes=[pltpu.VMEM((chunks, rows * group, LANES), f32)],
        input_output_aliases={} if scaled else {len(after) + len(parts) + 2: 0},
        cost_estimate=cost(
            6 * rows * count * group * depth * chunks * LANES,
            4 * rows * count * group * (2 * depth + chunks * LANES),
        ),
        name="y_inverse",
    )(scale, *parts, weight, base)


def update_body(step_ref, solution_ref, residual_ref, direction_ref, image_ref, one_ref, two_ref):
    step = step_ref[0]

    @pl.loop(0, one_ref.shape[0])
    def _(p):
        one_ref[p] = solution_ref[p] + step * direction_ref[p]
        two_ref[p] = residual_ref[p] - step * image_ref[p]


def update(step, solution, residual, direction, image, after=()):
    rows, columns, depth = solution.shape
    block = pl.BlockSpec((2, columns, depth), lambda g: (g, 0, 0))
    return ordered_call(
        update_body,
        after,
        grid=(rows // 2,),
        in_specs=[pl.BlockSpec(memory_space=pltpu.SMEM)] + [block] * 4,
        out_specs=[block] * 2,
        out_shape=[jax.ShapeDtypeStruct(solution.shape, f32)] * 2,
        cost_estimate=cost(4 * rows * columns * depth, 24 * rows * columns * depth),
        name="update",
    )(step, solution, residual, direction, image)


STRIDE = 4
RING = 3 * STRIDE


def image_body(blocks, coefficient_ref, front_ref, back_ref, own_ref, edge_ref, *refs):
    y_refs, (x_ref, direction_ref, reaction_ref) = refs[:blocks], refs[blocks : blocks + 3]
    image_ref, sum_ref, planes, mass_ring, stiff_ring = refs[blocks + 3 :]
    step, last = pl.program_id(0), pl.num_programs(0) - 1
    _, columns, depth = own_ref.shape
    edges = edge_ref.shape[1]
    tall = columns + edges

    def take(source):
        @pl.loop(0, STRIDE)
        def _(p):
            planes[pl.ds(pl.multiple_of(p * tall, 8), columns), :] = source[p]

    pl.when(step == 0)(lambda: take(front_ref))
    pl.when(step == last)(lambda: take(back_ref))
    pl.when(jnp.logical_and(step > 0, step < last))(lambda: take(own_ref))
    for p in range(STRIDE):
        planes[p * tall + columns : (p + 1) * tall, :] = edge_ref[p]

    high, low = halves(planes[...])
    mass, stiff = [], []
    for c in range(blocks):
        near = slice(max(c - 1, 0) * LANES, min(c + 2, blocks) * LANES)
        both = dot(
            jnp.concatenate([high[:, near], low[:, near], high[:, near]], axis=1), y_refs[c][...]
        )
        mass.append(both[:, :LANES])
        stiff.append(both[:, LANES:])
    mass, stiff = jnp.concatenate(mass, axis=1), jnp.concatenate(stiff, axis=1)
    stacked = jnp.concatenate(
        [
            jnp.concatenate([part[p * tall : (p + 1) * tall] for part in (mass, stiff)], axis=0)
            for p in range(STRIDE)
        ],
        axis=1,
    )
    high, low = halves(stacked)
    wide = dot(x_ref[...], high)
    result = (wide[: 2 * columns] + wide[2 * columns :]) + dot(x_ref[: 2 * columns, :], low)
    slot = lax.rem(step, 3) * STRIDE
    for p in range(STRIDE):
        mass_ring[slot + p] = result[:columns, p * depth : (p + 1) * depth]
        stiff_ring[slot + p] = result[columns:, p * depth : (p + 1) * depth]

    @pl.when(step == 0)
    def _():
        sum_ref[...] = jnp.zeros_like(sum_ref)

    @pl.when(step >= 2)
    def _():
        @pl.loop(0, STRIDE)
        def _(p):
            row = STRIDE * (step - 2) + p
            total = reaction_ref[p] * direction_ref[p]
            for o in range(7):
                place = lax.rem(row + o + STRIDE - 3, RING)
                total = total + (
                    coefficient_ref[row * 14 + o] * mass_ring[place]
                    + coefficient_ref[row * 14 + 7 + o] * stiff_ring[place]
                )
            image_ref[p] = total
            sum_ref[...] += folded(direction_ref[p] * total)


def neighbours(head, tail, axis):
    count = lax.axis_size(axis)
    even = lax.axis_index(axis) % 2 == 0
    received = []
    for first, sent in ((0, jnp.where(even, tail, head)), (1, jnp.where(even, head, tail))):
        pairs = [(i, i + 1) for i in range(first, count - 1, 2)]
        received.append(lax.ppermute(sent, axis, pairs + [(b, a) for a, b in pairs]))
    return jnp.where(even, received[1], received[0]), jnp.where(even, received[0], received[1])


def band_dense(row_bands, column_bands, row_at, column_at):
    distance = column_at[None, :] - row_at[:, None]
    total = jnp.zeros(distance.shape, f32)
    for k in range(4):
        total = jnp.where(distance == k, row_bands[k][:, None], total)
        if k:
            total = jnp.where(distance == -k, column_bands[k][None, :], total)
    return total


def apply_operator(direction, halos, reaction, time_bands, space_bands, after):
    rows, columns, depth = direction.shape
    blocks = depth // LANES
    plane = jnp.zeros((1, columns, depth), f32)
    before = jnp.concatenate([plane, halos[0]], axis=0)
    behind = jnp.concatenate([halos[1], plane], axis=0)

    def with_halos(part):
        return jnp.concatenate([part(halos[0]), part(direction), part(halos[1])], axis=0)

    edge = jnp.concatenate(
        neighbours(
            with_halos(lambda cells: cells[:, :3]),
            with_halos(lambda cells: cells[:, columns - 3 :]),
            "space",
        ),
        axis=1,
    )
    edge = jnp.pad(edge, ((1, 1), (0, 10), (0, 0)))
    whole = jnp.arange(depth)
    y_high, y_low = zip(
        *(
            halves_outside(band_dense(space_bands[m], space_bands[m], whole, whole))
            for m in (1, 0)
        )
    )
    y_parts = []
    for c in range(blocks):
        near = slice(max(c - 1, 0) * LANES, min(c + 2, blocks) * LANES)
        own = slice(c * LANES, (c + 1) * LANES)
        top, bottom = (
            jnp.concatenate([matrix[near, own] for matrix in matrices], axis=1)
            for matrices in (y_high, y_low)
        )
        y_parts.append(jnp.concatenate([top, top, bottom], axis=0))
    padded_space = jnp.pad(space_bands, ((0, 0), (0, 0), (3, 3)))
    near_x = lax.dynamic_slice_in_dim(
        padded_space, lax.axis_index("space") * columns, columns + 6, 2
    )
    row_at = jnp.arange(columns)
    column_at = jnp.concatenate(
        [row_at, jnp.arange(-3, 0), jnp.arange(columns, columns + 3), jnp.full((10,), -1000)]
    )
    x_columns = jnp.concatenate(
        [
            near_x[:, :, 3 : 3 + columns],
            near_x[:, :, :3],
            near_x[:, :, 3 + columns :],
            jnp.zeros((2, 4, 10), f32),
        ],
        axis=2,
    )
    x_stiff, x_mass = (
        band_dense(near_x[m, :, 3 : 3 + columns], x_columns[m], row_at, column_at)
        for m in (0, 1)
    )
    x_matrix = jnp.concatenate(
        [
            jnp.concatenate([x_mass, jnp.zeros_like(x_mass)], axis=1),
            jnp.concatenate([x_stiff, x_mass], axis=1),
        ],
        axis=0,
    )
    x_matrix = jnp.concatenate(halves_outside(x_matrix), axis=0)
    padded_time = jnp.pad(time_bands, ((0, 0), (0, 0), (3, 3)))
    near_t = lax.dynamic_slice_in_dim(padded_time, lax.axis_index("tm") * rows, rows + 6, 2)
    table = jnp.stack(
        [
            near_t[m, abs(o), 3 + min(o, 0) : 3 + min(o, 0) + rows]
            for m in (0, 1)
            for o in range(-3, 4)
        ],
        axis=1,
    ).reshape(-1)
    tall = columns + 16
    steps = rows // STRIDE + 2
    fixed = lambda array: pl.BlockSpec(array.shape, lambda g: (0,) * array.ndim)
    own = lambda late: pl.BlockSpec(
        (STRIDE, columns, depth), lambda g: (jnp.clip(g - late, 0, steps - 3), 0, 0)
    )
    return ordered_call(
        functools.partial(image_body, blocks),
        after,
        mib=56,
        grid=(steps,),
        in_specs=[pl.BlockSpec(memory_space=pltpu.SMEM), fixed(before), fixed(behind), own(1)]
        + [pl.BlockSpec((STRIDE, 16, depth), lambda g: (g, 0, 0))]
        + [fixed(part) for part in y_parts]
        + [fixed(x_matrix), own(2), own(2)],
        out_specs=[own(2), pl.BlockSpec((8, depth), lambda g: (0, 0))],
        out_shape=[
            jax.ShapeDtypeStruct((rows, columns, depth), f32),
            jax.ShapeDtypeStruct((8, depth), f32),
        ],
        scratch_shapes=[pltpu.VMEM((STRIDE * tall, depth), f32)]
        + [pltpu.VMEM((RING, columns, depth), f32)] * 2,
        cost_estimate=cost(
            12 * (rows + 6) * tall * depth * depth, 16 * rows * columns * depth
        ),
        name="image",
    )(table, before, behind, direction, edge, *y_parts, x_matrix, direction, reaction)


def by_xor(block, axis, k):
    return lax.ppermute(block, axis, [(j, j ^ k) for j in range(lax.axis_size(axis))])


def exchange(blocks, axis):
    count = len(blocks)
    received = {k: by_xor(blocks[k], axis, k) for k in range(count - 1, 0, -1)}
    return [blocks[0]] + [received[k] for k in range(1, count)]


def gathered_totals(scalars, label):
    row = lax.broadcasted_iota(jnp.int32, (8, LANES), 0)
    packed = jnp.zeros((8, LANES), f32)
    for i, scalar in enumerate(scalars):
        packed = jnp.where(row == i, scalar, packed)
    for axis in ("space", "tm"):
        count = lax.axis_size(axis)
        rounds = axis == "tm" or label == "total_a"
        packed = packed + by_xor(packed, axis, 1) if rounds else packed
        others = range(count - 2, 0, -2) if rounds else range(count - 1, 0, -1)
        parts = [packed] + [by_xor(packed, axis, k) for k in others]
        packed = sum(parts) if axis == "space" else packed
    return parts


def scale_body(old_ref, *refs):
    total = refs[0][...]
    for ref in refs[1:-1]:
        total = total + ref[...]
    refs[-1][...] = total / old_ref[0]


def scale_kernel(old, parts, after=()):
    return ordered_call(
        scale_body,
        after,
        in_specs=[pl.BlockSpec(memory_space=pltpu.SMEM)]
        + [pl.BlockSpec(memory_space=pltpu.VMEM)] * len(parts),
        out_specs=pl.BlockSpec(memory_space=pltpu.VMEM),
        out_shape=jax.ShapeDtypeStruct((8, LANES), f32),
        cost_estimate=cost(8 * LANES * len(parts), 4096 * len(parts)),
        name="scale",
    )(old, *parts)


def by_partner(values, axis, dim):
    count = lax.axis_size(axis)
    me = lax.axis_index(axis)
    return jnp.concatenate(
        [lax.dynamic_slice_in_dim(values, me ^ k, 1, dim) for k in range(count)], axis=dim
    )


def per_device(
    solution,
    residual,
    direction,
    reaction,
    time_bands,
    space_bands,
    time_basis,
    space_basis,
    time_eigen,
    space_eigen,
):
    rows, columns, depth = residual.shape
    group = lax.axis_size("tm")
    shares = lax.axis_size("space")
    me_t = lax.axis_index("tm")
    me_s = lax.axis_index("space")
    total = time_basis.shape[0]
    owned = total // shares
    width = LANES // group
    chunks = depth // LANES
    bundles = owned // group

    columns_first = by_partner(
        space_basis.T.reshape(chunks, group, width, depth), "tm", 1
    ).reshape(chunks, LANES, depth)
    y_high, y_low = halves_outside(columns_first)
    y_weights = jnp.concatenate([y_high, y_low], axis=1)
    y_weights = jnp.concatenate([y_weights, y_weights], axis=2)

    place = jnp.stack([me_t, me_s]).astype(jnp.int32)
    t_back = stacked_left(halves_outside(time_basis))
    t_ahead = stacked_left(halves_outside(time_basis.T))

    rows_first = (
        space_basis.reshape(shares, columns // group, group, depth)
        .transpose(2, 0, 1, 3)
        .reshape(shares * columns, depth)
    )
    x_back = stacked_left(halves_outside(rows_first))
    x_ahead = stacked_left(halves_outside(rows_first.T))

    own_time = lax.dynamic_slice_in_dim(time_eigen, me_s * owned, owned)
    own_space = lax.dynamic_slice_in_dim(
        space_eigen.reshape(chunks, group, width), me_t, 1, 1
    ).reshape(chunks, width)
    lane_eigen = (own_time[None, :, None] + own_space[:, None, :]).reshape(
        chunks, bundles // 2, 1, 2 * LANES
    )
    column_eigen = space_eigen[:, None]

    chain = []

    def kernel(call, *args):
        result = call(*args, chain[:])
        chain[:] = [result[0] if isinstance(result, (list, tuple)) else result]
        return result

    def y_ahead(field, k, name):
        blocks = kernel(y_forward, field, y_weights[k], group, 60 if name == "r" and k == 0 else 40)
        return exchange(blocks, "tm")

    def t_ahead_of(parts, pieces=1):
        blocks = kernel(t_forward, place, parts, t_ahead, shares, pieces)
        if pieces == 1:
            return exchange(blocks, "space")
        return [exchange(blocks[p * shares : (p + 1) * shares], "space") for p in range(pieces)]

    def x_first_of(parts, k):
        return kernel(x_first, place, parts, x_ahead, lane_eigen[k], column_eigen, group)

    def x_second_of(parts, k, piece=0, pieces=1):
        *blocks, part = kernel(
            x_second,
            place,
            step,
            parts,
            x_ahead,
            x_back,
            lane_eigen[k],
            column_eigen,
            first[k][0],
            group,
            piece * (bundles // 2 // pieces),
        )
        return exchange(blocks, "space"), jnp.sum(part)

    def t_back_of(parts, piece=0, pieces=1):
        blocks = kernel(t_inverse, place, parts, t_back, group, piece, pieces)
        return exchange(blocks, "tm")

    last = chunks - 1
    halos = neighbours(direction[:3], direction[rows - 3 :], "tm")
    sent = [y_ahead(residual, k, "r") for k in range(chunks)]
    image, curvature_parts = kernel(
        apply_operator, direction, halos, reaction, time_bands, space_bands
    )
    spread = [t_ahead_of(sent[0])]
    image_sent, first = [y_ahead(image, k, "i") for k in range(chunks)], []
    for k in range(1, chunks):
        spread.append(t_ahead_of(sent[k]))
        first.append(x_first_of(spread[k - 1], k - 1))
    first.append(x_first_of(spread[last], last))
    totals = sum(
        gathered_totals(
            (sum(jnp.sum(part) for _, part in first), jnp.sum(curvature_parts)), "total_a"
        )
    )
    norm_old, curvature = totals[0, 0], totals[1, 0]
    step_size = norm_old / curvature
    step = step_size.reshape(1)
    image_spread = [t_ahead_of(image_sent[0])]
    returned, back, sums = [], [], []
    pieces = 2 if bundles % 4 == 0 else 1
    for k in range(last):
        parts, part = x_second_of(image_spread[k], k)
        returned.append(parts)
        sums.append(part)
        if k == 0 and last > 1:
            image_spread.append(t_ahead_of(image_sent[1]))
            back.append(t_back_of(returned[0]))
        if k + 2 < last:
            image_spread.append(t_ahead_of(image_sent[k + 2]))
        if k == last - 1:
            image_spread.append(t_ahead_of(image_sent[last], pieces))
        if k >= len(back):
            back.append(t_back_of(returned[k]))
    ready = image_spread[last] if pieces > 1 else [image_spread[last]]
    returned_last = []
    for piece, parts in enumerate(ready):
        parts, part = x_second_of(parts, last, piece, pieces)
        returned_last += parts
        sums.append(part)
    new_parts = gathered_totals((sum(sums),), "total_b")
    back_last = t_back_of(returned_last)
    new_solution, new_residual = kernel(update, step, solution, residual, direction, image)
    scale = kernel(scale_kernel, norm_old.reshape(1), new_parts)[0, 0].reshape(1)
    partial = kernel(
        y_inverse,
        scale,
        [part for parts in back[:last] for part in parts],
        stacked_right([part[:last].reshape(last * LANES, depth) for part in (y_high, y_low)]),
        direction,
        group,
        True,
        0,
    )
    new_direction = y_inverse(
        scale, back_last, stacked_right((y_high[last], y_low[last])), partial, group, False
    )
    return (new_solution, new_residual, new_direction)


def solution(mesh):
    return jax.shard_map(
        per_device,
        mesh=mesh,
        in_specs=(
            P("tm", "space", None),
            P("tm", "space", None),
            P("tm", "space", None),
            P("tm", "space", None),
            P(),
            P(),
            P(),
            P(),
            P(),
            P(),
        ),
        out_specs=(P("tm", "space", None), P("tm", "space", None), P("tm", "space", None)),
        check_vma=False,
    )
```

```python
import functools

import jax
import jax.numpy as jnp
from jax import lax
from jax.experimental import pallas as pl
from jax.experimental.pallas import tpu as pltpu
from jax.sharding import PartitionSpec as P


LANES = 128
f32 = jnp.float32
bf16 = jnp.bfloat16


def cost(flops, nbytes):
    return pl.CostEstimate(flops=int(flops), bytes_accessed=int(nbytes), transcendentals=0)


def params(mib):
    return pltpu.CompilerParams(
        vmem_limit_bytes=mib * 1024 * 1024
    )


def ordered_call(body, after, in_specs, mib=40, **rest):
    def gated(*refs):
        return body(*refs[len(after) :])

    call = pl.pallas_call(
        gated,
        in_specs=[pl.BlockSpec(memory_space=pl.ANY)] * len(after) + list(in_specs),
        compiler_params=params(mib),
        **rest,
    )
    return lambda *args: call(*after, *args)


def halves(value):
    high = value.astype(bf16)
    return high, (value - high.astype(f32)).astype(bf16)


def halves_outside(value):
    high = lax.reduce_precision(value, 8, 7)
    return high.astype(bf16), (value - high).astype(bf16)


def dot(left, right):
    return jnp.dot(left, right, preferred_element_type=f32)


def dot_rows(left, right):
    return lax.dot_general(left, right, (((1,), (1,)), ((), ())), preferred_element_type=f32)


def stacked_left(parts):
    return jnp.concatenate([parts[0], parts[1], parts[0]], axis=1)


def stacked_right(parts):
    return jnp.concatenate([parts[0], parts[0], parts[1]], axis=0)


def swap_slots(arrays):
    count = len(arrays)
    width = LANES // count
    slot = lax.broadcasted_iota(jnp.int32, arrays[0].shape, 1) // width
    arrays = list(arrays)
    bit = 1
    while bit < count:
        upper = (slot & bit) != 0
        for i in range(count):
            if i & bit:
                continue
            low, high = arrays[i], arrays[i | bit]
            arrays[i] = jnp.where(upper, pltpu.roll(high, bit * width, 1), low)
            arrays[i | bit] = jnp.where(upper, high, pltpu.roll(low, LANES - bit * width, 1))
        bit *= 2
    return arrays


def y_forward_body(group, field_ref, weight_ref, *rest):
    outs, held = rest[:-1], rest[-1]
    rows, _, depth = field_ref.shape
    high, low = halves(field_ref[...].reshape(rows * group, depth))
    both = dot_rows(jnp.concatenate([high, low], axis=1), weight_ref[...])
    held[...] = both[:, :LANES] + both[:, LANES:]
    blocks = swap_slots([held[pl.ds(i, rows, stride=group), :] for i in range(group)])
    for out, block in zip(outs, blocks):
        out[0] = block


def y_forward(field, weight, group, mib, after=()):
    rows, columns, depth = field.shape
    count = columns // group
    return ordered_call(
        functools.partial(y_forward_body, group),
        after,
        mib=mib,
        grid=(count,),
        in_specs=[
            pl.BlockSpec((rows, group, depth), lambda g: (0, g, 0)),
            pl.BlockSpec((2 * LANES, 2 * depth), lambda g: (0, 0)),
        ],
        out_specs=[pl.BlockSpec((1, rows, LANES), lambda g: (g, 0, 0))] * group,
        out_shape=[jax.ShapeDtypeStruct((count, rows, LANES), f32)] * group,
        scratch_shapes=[pltpu.VMEM((rows * group, LANES), f32)],
        cost_estimate=cost(
            6 * rows * columns * depth * LANES, 4 * rows * columns * (depth + LANES)
        ),
        name="y_forward",
    )(field, weight)


def partner_rows(me, k, size, piece=0, pieces=1):
    share = size // pieces
    return pl.ds(pl.multiple_of((me ^ k) * size + piece * share, 8), share)


def t_forward_body(group, per_step, shares, place_ref, *refs):
    parts, weight_ref, outs = refs[:group], refs[group], refs[group + 1 : -1]
    held = refs[-1]
    rows, owned = held.shape[0] // group, held.shape[0] // shares
    for i in range(per_step):
        lanes = slice(i * LANES, (i + 1) * LANES)
        for e, part in enumerate(parts):
            held[partner_rows(place_ref[0], e, rows), lanes] = part[i]
    held[...] = dot(weight_ref[...], stacked_right(halves(held[...])))
    for i in range(per_step):
        lanes = slice(i * LANES, (i + 1) * LANES)
        pieces = len(outs) // shares
        for f, out in enumerate(outs):
            block = held[partner_rows(place_ref[1], f % shares, owned, f // shares, pieces), lanes]
            out[:, i * group : (i + 1) * group, :] = block.reshape(-1, group, LANES)


def t_forward(place, parts, weight, shares, pieces, after=()):
    group = len(parts)
    count, rows, _ = parts[0].shape
    total = weight.shape[0]
    bundles = total // shares // group // pieces
    per_step = 2 if count % 2 == 0 else 1
    return ordered_call(
        functools.partial(t_forward_body, group, per_step, shares),
        after,
        grid=(count // per_step,),
        in_specs=[pl.BlockSpec(memory_space=pltpu.SMEM)]
        + [pl.BlockSpec((per_step, rows, LANES), lambda g: (g, 0, 0))] * group
        + [pl.BlockSpec((total, 3 * total), lambda g: (0, 0))],
        out_specs=[pl.BlockSpec((bundles, per_step * group, LANES), lambda g: (0, g, 0))]
        * (shares * pieces),
        out_shape=[jax.ShapeDtypeStruct((bundles, count * group, LANES), f32)]
        * (shares * pieces),
        cost_estimate=cost(6 * total * total * count * LANES, 8 * total * count * LANES),
        scratch_shapes=[pltpu.VMEM((total, per_step * LANES), f32)],
        name="t_forward",
    )(place, *parts, weight)


def t_inverse_body(group, per_step, shares, halved, place_ref, *refs):
    count = shares * halved
    parts, weight_ref, outs = refs[:count], refs[count], refs[count + 1 : -1]
    held = refs[-1]
    rows, owned = held.shape[0] // group, held.shape[0] // shares
    for i in range(per_step):
        lanes = slice(i * LANES, (i + 1) * LANES)
        for f, part in enumerate(parts):
            rows_of = partner_rows(place_ref[1], f % shares, owned, f // shares, halved)
            held[rows_of, lanes] = part[:, i * group : (i + 1) * group, :].reshape(-1, LANES)
    held[...] = dot(weight_ref[...], stacked_right(halves(held[...])))
    for i in range(per_step):
        lanes = slice(i * LANES, (i + 1) * LANES)
        for e, out in enumerate(outs):
            out[i] = held[partner_rows(place_ref[0], e, rows), lanes]


def t_inverse(place, parts, weight, group, piece, pieces, after=()):
    shares = lax.axis_size("space")
    halved = len(parts) // shares
    bundles, lines, _ = parts[0].shape
    count = lines // group
    total = weight.shape[0]
    rows = total // group
    per_step = 2 if count % 2 == 0 else 1
    steps = count // per_step
    begin, end = (-(-steps * p // pieces) for p in (piece, piece + 1))
    count = (end - begin) * per_step
    return ordered_call(
        functools.partial(t_inverse_body, group, per_step, shares, halved),
        after,
        grid=(end - begin,),
        in_specs=[pl.BlockSpec(memory_space=pltpu.SMEM)]
        + [pl.BlockSpec((bundles, per_step * group, LANES), lambda g: (0, g + begin, 0))] * len(parts)
        + [pl.BlockSpec((total, 3 * total), lambda g: (0, 0))],
        out_specs=[pl.BlockSpec((per_step, rows, LANES), lambda g: (g, 0, 0))] * group,
        out_shape=[jax.ShapeDtypeStruct((count, rows, LANES), f32)] * group,
        cost_estimate=cost(6 * total * total * count * LANES, 8 * total * count * LANES),
        scratch_shapes=[pltpu.VMEM((total, per_step * LANES), f32)],
        name="t_inverse",
    )(place, *parts, weight)


def gathered(me, parts, held, group):
    lines = parts[0].shape[1]
    pieces = []
    for h in range(2):
        for f, part in enumerate(parts):
            held[partner_rows(me, f, lines), :] = part[h]
        spread = [
            held[pl.ds(i, held.shape[0] // group, stride=group), :] for i in range(group)
        ]
        pieces.append(jnp.concatenate(swap_slots(spread), axis=0))
    return jnp.concatenate(pieces, axis=1)


def folded(values):
    return values.reshape(values.shape[0] // 8, 8, values.shape[1]).sum(0)


def x_first_body(group, shares, place_ref, *refs):
    parts = refs[:shares]
    weight_ref, lane_ref, column_ref, hat_ref, sum_ref, held = refs[shares:]
    hat = dot(weight_ref[...], stacked_right(halves(gathered(place_ref[1], parts, held, group))))
    hat_ref[0] = hat
    eigen_sum = column_ref[...] + lane_ref[0]

    @pl.when(pl.program_id(0) == 0)
    def _():
        sum_ref[...] = jnp.zeros_like(sum_ref)

    sum_ref[...] += folded(hat * (hat / eigen_sum))


def x_first(place, parts, weight, lane_eigen, column_eigen, group, after=()):
    shares = len(parts)
    bundles, lines, _ = parts[0].shape
    wide = weight.shape[0]
    return ordered_call(
        functools.partial(x_first_body, group, shares),
        after,
        grid=(bundles // 2,),
        in_specs=[pl.BlockSpec(memory_space=pltpu.SMEM)]
        + [pl.BlockSpec((2, lines, LANES), lambda g: (g, 0, 0))] * shares
        + [pl.BlockSpec((wide, 3 * wide), lambda g: (0, 0))]
        + [
            pl.BlockSpec((1, 1, 2 * LANES), lambda g: (g, 0, 0)),
            pl.BlockSpec((wide, 1), lambda g: (0, 0)),
        ],
        out_specs=[
            pl.BlockSpec((1, wide, 2 * LANES), lambda g: (g, 0, 0)),
            pl.BlockSpec((8, 2 * LANES), lambda g: (0, 0)),
        ],
        out_shape=[
            jax.ShapeDtypeStruct((bundles // 2, wide, 2 * LANES), f32),
            jax.ShapeDtypeStruct((8, 2 * LANES), f32),
        ],
        scratch_shapes=[pltpu.VMEM((shares * lines, LANES), f32)],
        cost_estimate=cost(
            6 * wide * wide * bundles * LANES, 8 * wide * bundles * LANES
        ),
        name="x_first",
    )(place, *parts, weight, lane_eigen, column_eigen)


def x_second_body(group, shares, *refs):
    place_ref, step_ref, parts, refs = refs[0], refs[1], refs[2 : 2 + shares], refs[1:]
    forward_ref, back_ref, lane_ref, column_ref, hat_ref = refs[1 + shares : 6 + shares]
    outs, sum_ref, held = refs[6 + shares : -2], refs[-2], refs[-1]
    image_hat = dot(
        forward_ref[...], stacked_right(halves(gathered(place_ref[1], parts, held, group)))
    )
    new_hat = hat_ref[0] - step_ref[0] * image_hat
    spectral = new_hat / (column_ref[...] + lane_ref[0])

    @pl.when(pl.program_id(0) == 0)
    def _():
        sum_ref[...] = jnp.zeros_like(sum_ref)

    sum_ref[...] += folded(new_hat * spectral)
    back = dot(back_ref[...], stacked_right(halves(spectral)))
    lines = outs[0].shape[1]
    each = held.shape[0] // group
    for h in range(2):
        spread = swap_slots(
            [
                back[i * each : (i + 1) * each, h * LANES : (h + 1) * LANES]
                for i in range(group)
            ]
        )
        for i in range(group):
            held[pl.ds(i, each, stride=group), :] = spread[i]
        for f, out in enumerate(outs):
            out[h] = held[partner_rows(place_ref[1], f, lines), :]


def x_second(place, step, parts, forward, back, lane_eigen, column_eigen, hat, group, begin, after=()):
    shares = len(parts)
    bundles, lines, _ = parts[0].shape
    wide = forward.shape[0]
    return ordered_call(
        functools.partial(x_second_body, group, shares),
        after,
        grid=(bundles // 2,),
        in_specs=[pl.BlockSpec(memory_space=pltpu.SMEM)] * 2
        + [pl.BlockSpec((2, lines, LANES), lambda g: (g, 0, 0))] * shares
        + [pl.BlockSpec((wide, 3 * wide), lambda g: (0, 0))] * 2
        + [
            pl.BlockSpec((1, 1, 2 * LANES), lambda g: (g + begin, 0, 0)),
            pl.BlockSpec((wide, 1), lambda g: (0, 0)),
            pl.BlockSpec((1, wide, 2 * LANES), lambda g: (g + begin, 0, 0)),
        ],
        out_specs=[pl.BlockSpec((2, lines, LANES), lambda g: (g, 0, 0))] * shares
        + [pl.BlockSpec((8, 2 * LANES), lambda g: (0, 0))],
        out_shape=[jax.ShapeDtypeStruct((bundles, lines, LANES), f32)] * shares
        + [jax.ShapeDtypeStruct((8, 2 * LANES), f32)],
        scratch_shapes=[pltpu.VMEM((shares * lines, LANES), f32)],
        cost_estimate=cost(
            12 * wide * wide * bundles * LANES, 12 * wide * bundles * LANES
        ),
        name="x_second",
    )(place, step, *parts, forward, back, lane_eigen, column_eigen, hat)


def y_inverse_body(group, chunks, scaled, *refs):
    scale_ref = refs[0]
    parts = refs[1 : 1 + chunks * group]
    weight_ref, base_ref, out, held = refs[1 + chunks * group :]
    rows = parts[0].shape[1]
    for k in range(chunks):
        spread = swap_slots([part[0] for part in parts[k * group : (k + 1) * group]])
        for i in range(group):
            held[k, pl.ds(i, rows, stride=group), :] = spread[i]
    data = jnp.concatenate([held[k] for k in range(chunks)], axis=1)
    result = dot(stacked_left(halves(data)), weight_ref[...])
    result = result.reshape(out.shape)
    out[...] = result + (scale_ref[0] * base_ref[...] if scaled else base_ref[...])


def y_inverse(scale, parts, weight, base, group, scaled, begin=0, after=()):
    chunks = len(parts) // group
    count, rows, _ = parts[0].shape
    depth = weight.shape[1]
    block = pl.BlockSpec((rows, group, depth), lambda g: (0, g + begin, 0))
    return ordered_call(
        functools.partial(y_inverse_body, group, chunks, scaled),
        after,
        mib=60,
        grid=(count,),
        in_specs=[pl.BlockSpec(memory_space=pltpu.SMEM)]
        + [pl.BlockSpec((1, rows, LANES), lambda g: (g, 0, 0))] * len(parts)
        + [pl.BlockSpec((3 * chunks * LANES, depth), lambda g: (0, 0))]
        + [block],
        out_specs=block,
        out_shape=jax.ShapeDtypeStruct(base.shape, f32),
        scratch_shapes=[pltpu.VMEM((chunks, rows * group, LANES), f32)],
        input_output_aliases={} if scaled else {len(after) + len(parts) + 2: 0},
        cost_estimate=cost(
            6 * rows * count * group * depth * chunks * LANES,
            4 * rows * count * group * (2 * depth + chunks * LANES),
        ),
        name="y_inverse",
    )(scale, *parts, weight, base)


def update_body(step_ref, solution_ref, residual_ref, direction_ref, image_ref, one_ref, two_ref):
    step = step_ref[0]

    @pl.loop(0, one_ref.shape[0])
    def _(p):
        one_ref[p] = solution_ref[p] + step * direction_ref[p]
        two_ref[p] = residual_ref[p] - step * image_ref[p]


def update(step, solution, residual, direction, image, after=()):
    rows, columns, depth = solution.shape
    block = pl.BlockSpec((2, columns, depth), lambda g: (g, 0, 0))
    return ordered_call(
        update_body,
        after,
        grid=(rows // 2,),
        in_specs=[pl.BlockSpec(memory_space=pltpu.SMEM)] + [block] * 4,
        out_specs=[block] * 2,
        out_shape=[jax.ShapeDtypeStruct(solution.shape, f32)] * 2,
        cost_estimate=cost(4 * rows * columns * depth, 24 * rows * columns * depth),
        name="update",
    )(step, solution, residual, direction, image)


STRIDE = 4
RING = 3 * STRIDE


def image_body(blocks, coefficient_ref, front_ref, back_ref, own_ref, edge_ref, *refs):
    y_refs, (x_ref, direction_ref, reaction_ref) = refs[:blocks], refs[blocks : blocks + 3]
    image_ref, sum_ref, planes, mass_ring, stiff_ring = refs[blocks + 3 :]
    step, last = pl.program_id(0), pl.num_programs(0) - 1
    _, columns, depth = own_ref.shape
    edges = edge_ref.shape[1]
    tall = columns + edges

    def take(source):
        @pl.loop(0, STRIDE)
        def _(p):
            planes[pl.ds(pl.multiple_of(p * tall, 8), columns), :] = source[p]

    pl.when(step == 0)(lambda: take(front_ref))
    pl.when(step == last)(lambda: take(back_ref))
    pl.when(jnp.logical_and(step > 0, step < last))(lambda: take(own_ref))

    @pl.loop(0, STRIDE)
    def _(p):
        planes[pl.ds(pl.multiple_of(p * tall + columns, 8), edges), :] = edge_ref[p]

    high, low = halves(planes[...])
    mass, stiff = [], []
    for c in range(blocks):
        near = slice(max(c - 1, 0) * LANES, min(c + 2, blocks) * LANES)
        both = dot(
            jnp.concatenate([high[:, near], low[:, near], high[:, near]], axis=1), y_refs[c][...]
        )
        mass.append(both[:, :LANES])
        stiff.append(both[:, LANES:])
    mass, stiff = jnp.concatenate(mass, axis=1), jnp.concatenate(stiff, axis=1)
    stacked = jnp.concatenate(
        [
            jnp.concatenate([part[p * tall : (p + 1) * tall] for part in (mass, stiff)], axis=0)
            for p in range(STRIDE)
        ],
        axis=1,
    )
    high, low = halves(stacked)
    wide = dot(x_ref[...], high)
    result = (wide[: 2 * columns] + wide[2 * columns :]) + dot(x_ref[: 2 * columns, :], low)
    slot = lax.rem(step, 3) * STRIDE
    for p in range(STRIDE):
        mass_ring[slot + p] = result[:columns, p * depth : (p + 1) * depth]
        stiff_ring[slot + p] = result[columns:, p * depth : (p + 1) * depth]

    @pl.when(step == 0)
    def _():
        sum_ref[...] = jnp.zeros_like(sum_ref)

    @pl.when(step >= 2)
    def _():
        @pl.loop(0, STRIDE)
        def _(p):
            row = STRIDE * (step - 2) + p

            @pl.loop(0, columns // 16)
            def _(tile):
                lines = pl.ds(pl.multiple_of(tile * 16, 16), 16)
                own = direction_ref[p, lines, :]
                total = reaction_ref[p, lines, :] * own
                for o in range(7):
                    place = lax.rem(row + o + STRIDE - 3, RING)
                    total = total + (
                        coefficient_ref[row * 14 + o] * mass_ring[place, lines, :]
                        + coefficient_ref[row * 14 + 7 + o] * stiff_ring[place, lines, :]
                    )
                image_ref[p, lines, :] = total
                sum_ref[...] += folded(own * total)


def neighbours(head, tail, axis):
    count = lax.axis_size(axis)
    even = lax.axis_index(axis) % 2 == 0
    received = []
    for first, sent in ((0, jnp.where(even, tail, head)), (1, jnp.where(even, head, tail))):
        pairs = [(i, i + 1) for i in range(first, count - 1, 2)]
        received.append(lax.ppermute(sent, axis, pairs + [(b, a) for a, b in pairs]))
    return jnp.where(even, received[1], received[0]), jnp.where(even, received[0], received[1])


def band_dense(row_bands, column_bands, row_at, column_at):
    distance = column_at[None, :] - row_at[:, None]
    total = jnp.zeros(distance.shape, f32)
    for k in range(4):
        total = jnp.where(distance == k, row_bands[k][:, None], total)
        if k:
            total = jnp.where(distance == -k, column_bands[k][None, :], total)
    return total


def apply_operator(direction, halos, reaction, time_bands, space_bands, after):
    rows, columns, depth = direction.shape
    blocks = depth // LANES
    plane = jnp.zeros((1, columns, depth), f32)
    before = jnp.concatenate([plane, halos[0]], axis=0)
    behind = jnp.concatenate([halos[1], plane], axis=0)

    def with_halos(part):
        return jnp.concatenate([part(halos[0]), part(direction), part(halos[1])], axis=0)

    edge = jnp.concatenate(
        neighbours(
            with_halos(lambda cells: cells[:, :3]),
            with_halos(lambda cells: cells[:, columns - 3 :]),
            "space",
        ),
        axis=1,
    )
    edge = jnp.pad(edge, ((1, 1), (0, 10), (0, 0)))
    whole = jnp.arange(depth)
    y_high, y_low = zip(
        *(
            halves_outside(band_dense(space_bands[m], space_bands[m], whole, whole))
            for m in (1, 0)
        )
    )
    y_parts = []
    for c in range(blocks):
        near = slice(max(c - 1, 0) * LANES, min(c + 2, blocks) * LANES)
        own = slice(c * LANES, (c + 1) * LANES)
        top, bottom = (
            jnp.concatenate([matrix[near, own] for matrix in matrices], axis=1)
            for matrices in (y_high, y_low)
        )
        y_parts.append(jnp.concatenate([top, top, bottom], axis=0))
    padded_space = jnp.pad(space_bands, ((0, 0), (0, 0), (3, 3)))
    near_x = lax.dynamic_slice_in_dim(
        padded_space, lax.axis_index("space") * columns, columns + 6, 2
    )
    row_at = jnp.arange(columns)
    column_at = jnp.concatenate(
        [row_at, jnp.arange(-3, 0), jnp.arange(columns, columns + 3), jnp.full((10,), -1000)]
    )
    x_columns = jnp.concatenate(
        [
            near_x[:, :, 3 : 3 + columns],
            near_x[:, :, :3],
            near_x[:, :, 3 + columns :],
            jnp.zeros((2, 4, 10), f32),
        ],
        axis=2,
    )
    x_stiff, x_mass = (
        band_dense(near_x[m, :, 3 : 3 + columns], x_columns[m], row_at, column_at)
        for m in (0, 1)
    )
    x_matrix = jnp.concatenate(
        [
            jnp.concatenate([x_mass, jnp.zeros_like(x_mass)], axis=1),
            jnp.concatenate([x_stiff, x_mass], axis=1),
        ],
        axis=0,
    )
    x_matrix = jnp.concatenate(halves_outside(x_matrix), axis=0)
    padded_time = jnp.pad(time_bands, ((0, 0), (0, 0), (3, 3)))
    near_t = lax.dynamic_slice_in_dim(padded_time, lax.axis_index("tm") * rows, rows + 6, 2)
    table = jnp.stack(
        [
            near_t[m, abs(o), 3 + min(o, 0) : 3 + min(o, 0) + rows]
            for m in (0, 1)
            for o in range(-3, 4)
        ],
        axis=1,
    ).reshape(-1)
    tall = columns + 16
    steps = rows // STRIDE + 2
    fixed = lambda array: pl.BlockSpec(array.shape, lambda g: (0,) * array.ndim)
    own = lambda late: pl.BlockSpec(
        (STRIDE, columns, depth), lambda g: (jnp.clip(g - late, 0, steps - 3), 0, 0)
    )
    return ordered_call(
        functools.partial(image_body, blocks),
        after,
        mib=56,
        grid=(steps,),
        in_specs=[pl.BlockSpec(memory_space=pltpu.SMEM), fixed(before), fixed(behind), own(1)]
        + [pl.BlockSpec((STRIDE, 16, depth), lambda g: (g, 0, 0))]
        + [fixed(part) for part in y_parts]
        + [fixed(x_matrix), own(2), own(2)],
        out_specs=[own(2), pl.BlockSpec((8, depth), lambda g: (0, 0))],
        out_shape=[
            jax.ShapeDtypeStruct((rows, columns, depth), f32),
            jax.ShapeDtypeStruct((8, depth), f32),
        ],
        scratch_shapes=[pltpu.VMEM((STRIDE * tall, depth), f32)]
        + [pltpu.VMEM((RING, columns, depth), f32)] * 2,
        cost_estimate=cost(
            12 * (rows + 6) * tall * depth * depth, 16 * rows * columns * depth
        ),
        name="image",
    )(table, before, behind, direction, edge, *y_parts, x_matrix, direction, reaction)


def by_xor(block, axis, k):
    return lax.ppermute(block, axis, [(j, j ^ k) for j in range(lax.axis_size(axis))])


def exchange(blocks, axis):
    count = len(blocks)
    received = {k: by_xor(blocks[k], axis, k) for k in range(count - 1, 0, -1)}
    return [blocks[0]] + [received[k] for k in range(1, count)]


def gathered_totals(scalars, label):
    row = lax.broadcasted_iota(jnp.int32, (8, LANES), 0)
    packed = jnp.zeros((8, LANES), f32)
    for i, scalar in enumerate(scalars):
        packed = jnp.where(row == i, scalar, packed)
    for axis in ("space", "tm"):
        count = lax.axis_size(axis)
        rounds = axis == "tm" or label == "total_a"
        packed = packed + by_xor(packed, axis, 1) if rounds else packed
        others = range(count - 2, 0, -2) if rounds else range(count - 1, 0, -1)
        parts = [packed] + [by_xor(packed, axis, k) for k in others]
        packed = sum(parts) if axis == "space" else packed
    return parts


def scale_body(old_ref, *refs):
    total = refs[0][...]
    for ref in refs[1:-1]:
        total = total + ref[...]
    refs[-1][...] = total / old_ref[0]


def scale_kernel(old, parts, after=()):
    return ordered_call(
        scale_body,
        after,
        in_specs=[pl.BlockSpec(memory_space=pltpu.SMEM)]
        + [pl.BlockSpec(memory_space=pltpu.VMEM)] * len(parts),
        out_specs=pl.BlockSpec(memory_space=pltpu.VMEM),
        out_shape=jax.ShapeDtypeStruct((8, LANES), f32),
        cost_estimate=cost(8 * LANES * len(parts), 4096 * len(parts)),
        name="scale",
    )(old, *parts)


def by_partner(values, axis, dim):
    count = lax.axis_size(axis)
    me = lax.axis_index(axis)
    return jnp.concatenate(
        [lax.dynamic_slice_in_dim(values, me ^ k, 1, dim) for k in range(count)], axis=dim
    )


def per_device(
    solution,
    residual,
    direction,
    reaction,
    time_bands,
    space_bands,
    time_basis,
    space_basis,
    time_eigen,
    space_eigen,
):
    rows, columns, depth = residual.shape
    group = lax.axis_size("tm")
    shares = lax.axis_size("space")
    me_t = lax.axis_index("tm")
    me_s = lax.axis_index("space")
    total = time_basis.shape[0]
    owned = total // shares
    width = LANES // group
    chunks = depth // LANES
    bundles = owned // group

    columns_first = by_partner(
        space_basis.T.reshape(chunks, group, width, depth), "tm", 1
    ).reshape(chunks, LANES, depth)
    y_high, y_low = halves_outside(columns_first)
    y_weights = jnp.concatenate([y_high, y_low], axis=1)
    y_weights = jnp.concatenate([y_weights, y_weights], axis=2)

    place = jnp.stack([me_t, me_s]).astype(jnp.int32)
    t_back = stacked_left(halves_outside(time_basis))
    t_ahead = stacked_left(halves_outside(time_basis.T))

    rows_first = (
        space_basis.reshape(shares, columns // group, group, depth)
        .transpose(2, 0, 1, 3)
        .reshape(shares * columns, depth)
    )
    x_back = stacked_left(halves_outside(rows_first))
    x_ahead = stacked_left(halves_outside(rows_first.T))

    own_time = lax.dynamic_slice_in_dim(time_eigen, me_s * owned, owned)
    own_space = lax.dynamic_slice_in_dim(
        space_eigen.reshape(chunks, group, width), me_t, 1, 1
    ).reshape(chunks, width)
    lane_eigen = (own_time[None, :, None] + own_space[:, None, :]).reshape(
        chunks, bundles // 2, 1, 2 * LANES
    )
    column_eigen = space_eigen[:, None]

    chain = []

    def kernel(call, *args):
        result = call(*args, chain[:])
        chain[:] = [result[0] if isinstance(result, (list, tuple)) else result]
        return result

    def y_ahead(field, k, name):
        blocks = kernel(y_forward, field, y_weights[k], group, 60 if name == "r" and k == 0 else 40)
        return exchange(blocks, "tm")

    def t_ahead_of(parts, pieces=1):
        blocks = kernel(t_forward, place, parts, t_ahead, shares, pieces)
        if pieces == 1:
            return exchange(blocks, "space")
        return [exchange(blocks[p * shares : (p + 1) * shares], "space") for p in range(pieces)]

    def x_first_of(parts, k):
        return kernel(x_first, place, parts, x_ahead, lane_eigen[k], column_eigen, group)

    def x_second_of(parts, k, piece=0, pieces=1):
        *blocks, part = kernel(
            x_second,
            place,
            step,
            parts,
            x_ahead,
            x_back,
            lane_eigen[k],
            column_eigen,
            first[k][0],
            group,
            piece * (bundles // 2 // pieces),
        )
        return exchange(blocks, "space"), jnp.sum(part)

    def t_back_of(parts, piece=0, pieces=1):
        blocks = kernel(t_inverse, place, parts, t_back, group, piece, pieces)
        return exchange(blocks, "tm")

    last = chunks - 1
    halos = neighbours(direction[:3], direction[rows - 3 :], "tm")
    sent = [y_ahead(residual, k, "r") for k in range(chunks)]
    image, curvature_parts = kernel(
        apply_operator, direction, halos, reaction, time_bands, space_bands
    )
    spread = [t_ahead_of(sent[0])]
    image_sent, first = [y_ahead(image, k, "i") for k in range(chunks)], []
    for k in range(1, chunks):
        spread.append(t_ahead_of(sent[k]))
        first.append(x_first_of(spread[k - 1], k - 1))
    first.append(x_first_of(spread[last], last))
    totals = sum(
        gathered_totals(
            (sum(jnp.sum(part) for _, part in first), jnp.sum(curvature_parts)), "total_a"
        )
    )
    norm_old, curvature = totals[0, 0], totals[1, 0]
    step_size = norm_old / curvature
    step = step_size.reshape(1)
    image_spread = [t_ahead_of(image_sent[0])]
    returned, back, sums = [], [], []
    pieces = 2 if bundles % 4 == 0 else 1
    for k in range(last):
        parts, part = x_second_of(image_spread[k], k)
        returned.append(parts)
        sums.append(part)
        if k == 0 and last > 1:
            image_spread.append(t_ahead_of(image_sent[1]))
            back.append(t_back_of(returned[0]))
        if k + 2 < last:
            image_spread.append(t_ahead_of(image_sent[k + 2]))
        if k == last - 1:
            image_spread.append(t_ahead_of(image_sent[last], pieces))
        if k >= len(back):
            back.append(t_back_of(returned[k]))
    ready = image_spread[last] if pieces > 1 else [image_spread[last]]
    returned_last = []
    for piece, parts in enumerate(ready):
        parts, part = x_second_of(parts, last, piece, pieces)
        returned_last += parts
        sums.append(part)
    new_parts = gathered_totals((sum(sums),), "total_b")
    back_last = t_back_of(returned_last)
    new_solution, new_residual = kernel(update, step, solution, residual, direction, image)
    scale = kernel(scale_kernel, norm_old.reshape(1), new_parts)[0, 0].reshape(1)
    partial = kernel(
        y_inverse,
        scale,
        [part for parts in back[:last] for part in parts],
        stacked_right([part[:last].reshape(last * LANES, depth) for part in (y_high, y_low)]),
        direction,
        group,
        True,
        0,
    )
    new_direction = y_inverse(
        scale, back_last, stacked_right((y_high[last], y_low[last])), partial, group, False
    )
    return (new_solution, new_residual, new_direction)


def solution(mesh):
    return jax.shard_map(
        per_device,
        mesh=mesh,
        in_specs=(
            P("tm", "space", None),
            P("tm", "space", None),
            P("tm", "space", None),
            P("tm", "space", None),
            P(),
            P(),
            P(),
            P(),
            P(),
            P(),
        ),
        out_specs=(P("tm", "space", None), P("tm", "space", None), P("tm", "space", None)),
        check_vma=False,
    )
```
